128 devices in a mesh: row: 8 (over x, core), col: 16 (over y, z).
Axes of the slice: x: 4, y: 4, z: 4, core: 2. Of those that a mesh axis runs over, the one named last changes fastest.
Arguments:
- coupling: bfloat16 [128, 4096, 1024], P(('row', 'col')), may hold values from -0.09375 to 0.09375
- modes: bfloat16 [128, 200, 4096], P(('row', 'col')), may hold values from -6 to 6
- flexibility: float32 [128, 200], P(('row', 'col')), may hold values from 0.002 to 0.02
- widths: int32 [128], P(('row', 'col')), may hold values from 512 to 1024
- segments: int32 [128, 8], replicated, may hold values from 0 to 95, as said below
Outputs:
- interface: float32 [12288, 12288], P('row', 'col')
The draws below stay inside these ranges and needn't reach their ends.
Inputs may be any that keep to these rules, and one draw needn't show every extreme that they name: `segments`: the 8 segment numbers of a substructure are distinct, and modulo 16 they are 8 cyclically consecutive residues. `widths`: columns at and beyond a substructure's width are padding.
All inputs are finite; a program needn't handle non-finite values.
Results may differ from the reference program's by a relative error of at most 0.0003.
Values sent between devices are 32-bit elements; how exact they have to be, the bound alone decides.
A program may use at most 192 MiB of HBM per device.

```python
import math
import jax
import jax.numpy as jnp
from jax import lax

NI = 4096
NB = 1024
MODES = 200
TILE = 128
NG = 12288
RESIDUE_GROUPS = 16
SUBSTRUCT_TOTAL = 128
SEGMENTS_PER_SUB = 8
SEGMENT_TOTAL = 96
N_ROW = 8
N_COL = 16


def draw_segments(key, part):
    first, second_member = jax.random.split(jax.random.fold_in(key, 7))
    start_shift = jax.random.randint(first, (SUBSTRUCT_TOTAL, 1), 0, RESIDUE_GROUPS)
    tree_level = jax.random.randint(second_member, (SUBSTRUCT_TOTAL, SEGMENTS_PER_SUB), 0, SEGMENT_TOTAL // RESIDUE_GROUPS)
    residue_class = (jnp.arange(SEGMENTS_PER_SUB, dtype=jnp.int32)[None, :] + start_shift) % RESIDUE_GROUPS
    return (residue_class + RESIDUE_GROUPS * tree_level).astype(jnp.int32)


def touch_ends(result, rng, low, top_value):
    dims = result.shape
    spot = [jax.random.randint(jax.random.fold_in(rng, axis), (), 0, dims[axis]) for axis in range(len(dims))]
    result = result.at[tuple(spot)].set(low)
    longest = dims.index(max(dims))
    spot[longest] = (spot[longest] + 1) % dims[longest]
    return result.at[tuple(spot)].set(top_value)


def shard_levels(own_key, dims, cuts, least, top_value):
    def one(dim, parts):
        draws = jax.random.uniform(jax.random.fold_in(jax.random.fold_in(own_key, 6), dim), (parts,), jnp.float32, least / len(cuts), top_value / len(cuts))
        return jnp.repeat(jnp.exp(draws), dims[dim] // parts).reshape((-1,) + (1,) * (len(dims) - dim - 1))

    factor_of = one(*cuts[0])
    for cut in cuts[1:]:
        factor_of = factor_of * one(*cut)
    return factor_of


def noise(key, dims, scale, most, cuts=(), kind=jnp.bfloat16):
    array = jax.random.normal(key, dims, jnp.float32) * scale
    if len(cuts) > 0:
        array = shard_levels(key, dims, cuts, -0.22, 0.18) * array
    return jnp.clip(array, min=-most, max=most).astype(kind)


def setup_inputs(seed: int = 0) -> dict:
    seeds = jax.random.split(jax.random.key(seed), 6)
    coupling = noise(seeds[0], (SUBSTRUCT_TOTAL, NI, NB), NI ** -0.5, 0.09375, ((0, 128),))
    modes = noise(seeds[1], (SUBSTRUCT_TOTAL, MODES, NI), 1.0, 6.0, ((0, 128),))
    flexibility = jnp.clip(jnp.exp(math.log(0.02) - 2.30258502 * jax.random.uniform(seeds[2], (SUBSTRUCT_TOTAL, MODES), jnp.float32) ** shard_levels(seeds[2], (SUBSTRUCT_TOTAL, MODES), ((0, 128),), -0.2, 0.2)), 0.002, 0.02)
    widths = touch_ends(jax.random.randint(seeds[3], (SUBSTRUCT_TOTAL,), NB // 2, NB + 1), jax.random.fold_in(seeds[3], 1), NB // 2, NB).astype(jnp.int32)
    segments = draw_segments(jax.random.fold_in(seeds[5], 71), 0)
    return {"coupling": coupling, "modes": modes, "flexibility": flexibility, "widths": widths, "segments": segments}


def substructure_block(factor, modal_rows, weights, width):
    padded = factor.shape[1]
    columns = lax.broadcasted_iota(jnp.int32, (1, padded), 1)
    masked = jnp.where(columns < width, factor, jnp.zeros((), factor.dtype))
    static = lax.dot_general(masked, masked, (((0,), (0,)), ((), ())), preferred_element_type=jnp.float32)
    projected = jnp.dot(modal_rows, masked, preferred_element_type=jnp.float32)
    modal = lax.dot_general(projected * weights[:, None], projected, (((0,), (0,)), ((), ())), precision=lax.Precision.HIGHEST, preferred_element_type=jnp.float32)
    return static - modal

def reference(coupling, modes, flexibility, widths, segments):
    subs_total = coupling.shape[0]
    seg_count = coupling.shape[2] // TILE
    seg_total = NG // TILE

    def add_one(member, matrix):
        block = substructure_block(coupling[member], modes[member], flexibility[member], widths[member])
        tiles = block.reshape(seg_count, TILE, seg_count, TILE).transpose(0, 2, 1, 3)
        placed = segments[member].astype(jnp.int32)
        return matrix.at[placed[:, None], placed[None, :]].add(tiles)
    start = jnp.zeros((seg_total, seg_total, TILE, TILE), jnp.float32)
    matrix = lax.fori_loop(0, subs_total, add_one, start)
    ordinal = jnp.arange(seg_total)
    diag_tiles = matrix[ordinal, ordinal]
    diag_values = jnp.diagonal(diag_tiles, axis1=1, axis2=2)
    scale = 1.0 / jnp.sqrt(1.0 + jnp.abs(diag_values))
    scaled = matrix * scale[:, None, :, None] * scale[None, :, None, :]
    row_order = jnp.arange(seg_total).reshape(seg_total // N_ROW, N_ROW).T.reshape(-1)
    col_order = jnp.arange(seg_total).reshape(seg_total // N_COL, N_COL).T.reshape(-1)
    ordered = scaled[row_order][:, col_order]
    return ordered.transpose(0, 2, 1, 3).reshape(NG, NG)
```

```python
import functools

import jax
import jax.numpy as jnp
from jax import lax
from jax.experimental import pallas as pl
from jax.experimental.pallas import tpu as pltpu
from jax.sharding import PartitionSpec as P

TILE = 128
CHUNKS = 4
PART = TILE // CHUNKS
CLASSES = 8
PLANE = 32
RING = 4
ROW_TILES = 12
COL_TILES = 6
DEPTH = 1024
F32 = jnp.float32
BF16 = jnp.bfloat16
MESH = pl.DeviceIdType.MESH
HIGH = lax.Precision.HIGHEST


def over_rows(left, right):
    return lax.dot_general(left, right, (((0,), (0,)), ((), ())), preferred_element_type=F32)


def block_kernel(steps, perm, width, *refs):
    columns, (modes, weights, out, diag, masked, acc, proj) = refs[:CLASSES], refs[CLASSES:]
    step = pl.program_id(0)
    for k in range(CLASSES):
        lane = lax.broadcasted_iota(jnp.int32, (DEPTH, TILE), 1) + perm[k] * TILE
        masked[:, k * TILE : (k + 1) * TILE] = jnp.where(
            lane < width[0], columns[k][0], jnp.zeros((), BF16)
        )

    @pl.when(step == 0)
    def _():
        acc[...] = jnp.zeros_like(acc)
        proj[...] = jnp.zeros_like(proj)

    proj[...] += jnp.dot(modes[0], masked[...], preferred_element_type=F32)
    for m in range(0, 1024, 256):
        acc[m : m + 256, m:] += over_rows(masked[:, m : m + 256], masked[:, m:])

    @pl.when(step == steps - 1)
    def _():
        p = proj[...]
        w = p * weights[...]
        p_hi, w_hi = p.astype(BF16), w.astype(BF16)
        p_lo = (p - p_hi.astype(F32)).astype(BF16)
        w_lo = (w - w_hi.astype(F32)).astype(BF16)
        left = jnp.concatenate([w_hi, w_hi, w_lo], 0)
        right = jnp.concatenate([p_hi, p_lo, p_hi], 0)
        for m in range(0, 1024, 256):
            acc[m : m + 256, m:] -= over_rows(left[:, m : m + 256], right[:, m:])
        for m in range(256, 1024, 256):
            for n in range(0, m, 256):
                acc[m : m + 256, n : n + 256] = acc[n : n + 256, m : m + 256].T
        same = lax.broadcasted_iota(jnp.int32, (TILE, TILE), 0) == lax.broadcasted_iota(
            jnp.int32, (TILE, TILE), 1
        )
        for k in range(CLASSES):
            for m in range(CLASSES):
                for q in range(CHUNKS):
                    rows = k * TILE + q * PART
                    out[q, k, m % 4, m // 4] = acc[rows : rows + PART, m * TILE : (m + 1) * TILE]
            tile = acc[k * TILE : (k + 1) * TILE, k * TILE : (k + 1) * TILE]
            diag[k : k + 1, :] = jnp.sum(jnp.where(same, tile, 0.0), axis=0, keepdims=True)


def make_block(coupling, modes, flexibility, width, perm):
    steps = coupling.shape[1] // DEPTH
    count = modes.shape[1]

    def column(k, i, perm, width):
        return (0, i, perm[k])

    return pl.pallas_call(
        functools.partial(block_kernel, steps),
        grid_spec=pltpu.PrefetchScalarGridSpec(
            num_scalar_prefetch=2,
            grid=(steps,),
            in_specs=[
                pl.BlockSpec((1, DEPTH, TILE), functools.partial(column, k)) for k in range(CLASSES)
            ]
            + [
                pl.BlockSpec((1, count, DEPTH), lambda i, perm, width: (0, 0, i)),
                pl.BlockSpec((count, 1), lambda i, perm, width: (0, 0)),
            ],
            out_specs=[
                pl.BlockSpec((CHUNKS, 8, 4, 2, PART, TILE), lambda i, perm, width: (0,) * 6),
                pl.BlockSpec((CLASSES, TILE), lambda i, perm, width: (0, 0)),
            ],
            scratch_shapes=[
                pltpu.VMEM((DEPTH, 1024), BF16),
                pltpu.VMEM((1024, 1024), F32),
                pltpu.VMEM((count, 1024), F32),
            ],
        ),
        out_shape=[
            jax.ShapeDtypeStruct((CHUNKS, 8, 4, 2, PART, TILE), F32),
            jax.ShapeDtypeStruct((CLASSES, TILE), F32),
        ],
        compiler_params=pltpu.CompilerParams(vmem_limit_bytes=48 << 20),
        name="block",
    )(perm, width, *([coupling] * CLASSES), modes, flexibility.reshape(count, 1))


def exchange_kernel(cap, order, tiles, diag, ring_out, own_out, diag_out, *scratch):
    held, scratch = scratch[:CHUNKS], scratch[CHUNKS:]
    send, diag_held, diag_send, a_send, a_recv, b_send, b_recv, o_sem, d_sem = scratch
    row, col = lax.axis_index("row"), lax.axis_index("col")
    y, z = col // 4, col % 4
    mine = row * 4 + z

    def plane_peer(step):
        there = lax.rem(mine + step, PLANE)
        return there, (there // 4, y * 4 + lax.rem(there, 4))

    def ring_peer(step):
        return (row, lax.rem(y + step, RING) * 4 + z)

    barrier = pltpu.get_barrier_semaphore()

    def greet(step, carry):
        pl.semaphore_signal(barrier, inc=1, device_id=plane_peer(step)[1], device_id_type=MESH)
        return carry

    lax.fori_loop(1, PLANE, greet, 0)
    for step in range(1, RING):
        pl.semaphore_signal(barrier, inc=1, device_id=ring_peer(step), device_id_type=MESH)
    pl.semaphore_wait(barrier, PLANE - 1 + RING - 1)

    own_copies = []

    def local(src, dst, sem):
        copy = pltpu.make_async_copy(src, dst, sem)
        copy.start()
        return copy

    def send_diag(step, carry):
        pltpu.make_async_remote_copy(
            src_ref=diag,
            dst_ref=diag_held.at[mine],
            send_sem=d_sem.at[0],
            recv_sem=d_sem.at[1],
            device_id=plane_peer(step)[1],
            device_id_type=MESH,
        ).start()
        return carry

    lax.fori_loop(1, PLANE, send_diag, 0)
    own_diag = local(diag, diag_held.at[mine], d_sem.at[2])
    for q in range(CHUNKS):

        def send_tiles(step, carry, q=q):
            there, peer = plane_peer(step)
            pltpu.make_async_remote_copy(
                src_ref=tiles.at[q, there // 4, lax.rem(there, 4)],
                dst_ref=held[q].at[mine],
                send_sem=a_send.at[q],
                recv_sem=a_recv.at[q],
                device_id=peer,
                device_id_type=MESH,
            ).start()
            return carry

        lax.fori_loop(1, PLANE, send_tiles, 0)
        own_copies.append(local(tiles.at[q, row, z], held[q].at[mine], o_sem.at[0, q]))

    def whole(ref, sem):
        part = ref.at[pl.ds(0, PLANE - 1)]
        pltpu.make_async_copy(part, part, sem).wait()

    pending = []
    whole(diag_held, d_sem.at[1])
    own_diag.wait()

    def pick(i, carry):
        for parity in range(2):
            diag_send[parity, 0, pl.ds(i, 1), :] = diag_held[i, pl.ds(row, 1), :]
            diag_send[parity, 1, pl.ds(i, 1), :] = diag_held[i, pl.ds(4 * parity + z, 1), :]
        return carry

    lax.fori_loop(0, PLANE, pick, 0)
    here = local(diag_send.at[lax.rem(y, 2)], diag_out.at[0], d_sem.at[3])
    for step in range(1, RING):
        copy = pltpu.make_async_remote_copy(
            src_ref=diag_send.at[lax.rem(y + step, 2)],
            dst_ref=diag_out.at[step],
            send_sem=b_send.at[CHUNKS, step - 1],
            recv_sem=b_recv.at[CHUNKS, step - 1],
            device_id=ring_peer(step),
            device_id_type=MESH,
        )
        copy.start()
        pending.append(copy)
    for q in range(CHUNKS):
        whole(held[q], a_recv.at[q])
        own_copies[q].wait()
        for step in range(1, RING):
            parity = lax.rem(y + step, 2)

            def arrange(j, carry, q=q, step=step, parity=parity):
                send[q, step - 1, j] = held[q][order[step - 1, j], parity]
                return carry

            lax.fori_loop(0, cap, arrange, 0)
            copy = pltpu.make_async_remote_copy(
                src_ref=send.at[q, step - 1],
                dst_ref=ring_out.at[q, step - 1, pl.ds(0, cap)],
                send_sem=b_send.at[q, step - 1],
                recv_sem=b_recv.at[q, step - 1],
                device_id=ring_peer(step),
                device_id_type=MESH,
            )
            copy.start()
            pending.append(copy)
        own_copies[q] = local(held[q].at[:, lax.rem(y, 2)], own_out.at[q], o_sem.at[1, q])
    for copy in pending:
        copy.wait()
    for copy in own_copies:
        copy.wait()
    here.wait()
    whole(diag_held, d_sem.at[0])
    for q in range(CHUNKS):
        whole(held[q], a_send.at[q])


def exchange(cap, order, tiles, diag):
    dma = pltpu.SemaphoreType.DMA
    anywhere = pl.BlockSpec(memory_space=pl.ANY)
    return pl.pallas_call(
        functools.partial(exchange_kernel, cap),
        in_specs=[pl.BlockSpec(memory_space=pltpu.SMEM), anywhere, anywhere],
        out_specs=[anywhere] * 3,
        out_shape=[
            jax.ShapeDtypeStruct((CHUNKS, RING - 1, PLANE, PART, TILE), F32),
            jax.ShapeDtypeStruct((CHUNKS, PLANE, PART, TILE), F32),
            jax.ShapeDtypeStruct((RING, 2, PLANE, TILE), F32),
        ],
        scratch_shapes=[pltpu.VMEM((PLANE, 2, PART, TILE), F32)] * CHUNKS
        + [
            pltpu.VMEM((CHUNKS, RING - 1, cap, PART, TILE), F32),
            pltpu.VMEM((PLANE, CLASSES, TILE), F32),
            pltpu.VMEM((2, 2, PLANE, TILE), F32),
            dma((CHUNKS,)),
            dma((CHUNKS,)),
            dma((CHUNKS + 1, RING - 1)),
            dma((CHUNKS + 1, RING - 1)),
            dma((2, CHUNKS)),
            dma((4,)),
        ],
        compiler_params=pltpu.CompilerParams(
            collective_id=cap, has_side_effects=True, vmem_limit_bytes=40 << 20
        ),
        name="exchange",
    )(order, tiles, diag)


def assemble_kernel(count, place, ring, own, diag, row_hot, col_hot, out, row_scale, col_scale):
    chunk = pl.program_id(0)

    @pl.when(chunk == 0)
    def _():
        rows = lax.dot_general(
            diag[:, 0].reshape(RING * PLANE, TILE),
            row_hot[...],
            (((0,), (0,)), ((), ())),
            precision=HIGH,
            preferred_element_type=F32,
        )
        cols = jnp.dot(
            col_hot[...],
            diag[:, 1].reshape(RING * PLANE, TILE),
            precision=HIGH,
            preferred_element_type=F32,
        )
        row_scale[...] = 1.0 / jnp.sqrt(1.0 + jnp.abs(rows))
        col_scale[...] = 1.0 / jnp.sqrt(1.0 + jnp.abs(cols))

    out[...] = jnp.zeros_like(out)
    for d in range(RING):

        def add(j, carry, d=d):
            code = place[d, j]
            tile = own[0, code & 31] if d == 0 else ring[0, d - 1, j]
            across = pl.ds(pl.multiple_of((code >> 9) * TILE, TILE), TILE)
            out[(code >> 5) & 15, 0, :, across] += tile
            return carry

        lax.fori_loop(0, count[d], add, 0)
    inside = pl.ds(pl.multiple_of(chunk * PART, PART), PART)
    for g in range(ROW_TILES):
        for h in range(COL_TILES):
            scale = row_scale[inside, g : g + 1] * col_scale[h : h + 1, :]
            out[g, 0, :, h * TILE : (h + 1) * TILE] *= scale


def assemble(cap, count, place, ring, own, diag, row_hot, col_hot):
    return pl.pallas_call(
        assemble_kernel,
        grid_spec=pltpu.PrefetchScalarGridSpec(
            num_scalar_prefetch=2,
            grid=(CHUNKS,),
            in_specs=[
                pl.BlockSpec((1, RING - 1, cap, PART, TILE), lambda q, n, p: (q, 0, 0, 0, 0)),
                pl.BlockSpec((1, PLANE, PART, TILE), lambda q, n, p: (q, 0, 0, 0)),
                pl.BlockSpec((RING, 2, PLANE, TILE), lambda q, n, p: (0, 0, 0, 0)),
                pl.BlockSpec((RING * PLANE, 16), lambda q, n, p: (0, 0)),
                pl.BlockSpec((8, RING * PLANE), lambda q, n, p: (0, 0)),
            ],
            out_specs=pl.BlockSpec(
                (ROW_TILES, 1, PART, COL_TILES * TILE), lambda q, n, p: (0, q, 0, 0)
            ),
            scratch_shapes=[pltpu.VMEM((TILE, 16), F32), pltpu.VMEM((8, TILE), F32)],
        ),
        out_shape=jax.ShapeDtypeStruct((ROW_TILES, CHUNKS, PART, COL_TILES * TILE), F32),
        compiler_params=pltpu.CompilerParams(vmem_limit_bytes=40 << 20),
        name="assemble",
    )(count, place, ring, own, diag, row_hot, col_hot)


def sum_where(mask, values, axis):
    return jnp.sum(jnp.where(mask, values, 0), axis=axis)


def places(segments, row, col):
    y, z = col // 4, col % 4
    iota8 = jnp.arange(8, dtype=jnp.int32)
    slots = jnp.arange(PLANE, dtype=jnp.int32)
    steps = jnp.arange(RING, dtype=jnp.int32)
    in_class = (segments & 7)[:, :, None] == iota8
    by_class = sum_where(in_class, segments[:, :, None], 1)
    mine = jnp.arange(128, dtype=jnp.int32)[:, None] == row * 16 + col
    perm = sum_where(in_class & mine[:, :, None], iota8[None, :, None], (0, 1))
    planes = by_class.reshape(8, RING, 4, 8)
    ring = (y - steps) & 3
    from_plane = ring[:, None, None, None, None] == steps[None, None, :, None, None]
    held = sum_where(from_plane, planes[None], 2).reshape(RING, PLANE, 8)
    row_seg = sum_where(iota8 == row, held, 2)
    col_seg = sum_where(iota8 == (col & 7), held, 2)
    goes = (y + steps) & 3
    out_seg = sum_where(iota8 == (4 * (goes & 1) + z)[:, None, None], held[:1], 2)
    arrives = ((col_seg >> 3) & 1) == (col >> 3)
    leaves = ((out_seg >> 3) & 1) == (goes >> 1)[:, None]
    flags = jnp.stack([arrives, leaves])
    before = slots[:, None] > slots[None, :]
    rank = jnp.sum((flags[:, :, None, :] & before).astype(jnp.int32), axis=3)
    lands = flags[:, :, None, :] & (rank[:, :, None, :] == slots[:, None])
    codes = slots + 32 * (row_seg >> 3) + 512 * (col_seg >> 4)
    values = jnp.stack([codes, jnp.broadcast_to(slots, codes.shape)])
    table = sum_where(lands, values[:, :, None, :], 3)
    count = jnp.sum(arrives.astype(jnp.int32), axis=1)
    row_hot = (row_seg.reshape(-1)[:, None] >> 3) == jnp.arange(16, dtype=jnp.int32)
    col_place = jnp.where(arrives, col_seg >> 4, -1).reshape(-1)
    col_hot = col_place[None, :] == iota8[:, None]
    return perm, table[1, 1:], count, table[0], row_hot.astype(F32), col_hot.astype(F32)


def body(coupling, modes, flexibility, widths, segments):
    row, col = lax.axis_index("row"), lax.axis_index("col")
    perm, order, count, place, row_hot, col_hot = places(segments, row, col)
    tiles, diag = make_block(coupling, modes, flexibility[0], widths, perm)
    ring, own, diags = exchange(PLANE, order, tiles, diag)
    out = assemble(PLANE, count, place, ring, own, diags, row_hot, col_hot)
    return out.reshape(ROW_TILES * TILE, COL_TILES * TILE)


def solution(mesh):
    both = ("row", "col")
    return jax.shard_map(
        body,
        mesh=mesh,
        in_specs=(P(both, None, None), P(both, None, None), P(both, None), P(both), P()),
        out_specs=P("row", "col"),
        check_vma=False,
    )
```

```python
import functools

import jax
import jax.numpy as jnp
from jax import lax
from jax.experimental import pallas as pl
from jax.experimental.pallas import tpu as pltpu
from jax.sharding import PartitionSpec as P

TILE = 128
CHUNKS = 8
PART = TILE // CHUNKS
CLASSES = 8
PLANE = 32
RING = 4
ROW_TILES = 12
COL_TILES = 6
DEPTH = 1024
CAPS = (20, 22, 24, PLANE)
F32 = jnp.float32
BF16 = jnp.bfloat16
MESH = pl.DeviceIdType.MESH
HIGH = lax.Precision.HIGHEST


def over_rows(left, right):
    return lax.dot_general(left, right, (((0,), (0,)), ((), ())), preferred_element_type=F32)


def block_kernel(steps, perm, width, *refs):
    columns, (modes, weights, out, diag, masked, acc, proj) = refs[:CLASSES], refs[CLASSES:]
    step = pl.program_id(0)
    for k in range(CLASSES):
        lane = lax.broadcasted_iota(jnp.int32, (DEPTH, TILE), 1) + perm[k] * TILE
        masked[:, k * TILE : (k + 1) * TILE] = jnp.where(
            lane < width[0], columns[k][0], jnp.zeros((), BF16)
        )

    @pl.when(step == 0)
    def _():
        acc[...] = jnp.zeros_like(acc)
        proj[...] = jnp.zeros_like(proj)

    proj[...] += jnp.dot(modes[0], masked[...], preferred_element_type=F32)
    for m in range(0, 1024, 256):
        acc[m : m + 256, m:] += over_rows(masked[:, m : m + 256], masked[:, m:])

    @pl.when(step == steps - 1)
    def _():
        p = proj[...]
        w = p * weights[...]
        p_hi, w_hi = p.astype(BF16), w.astype(BF16)
        p_lo = (p - p_hi.astype(F32)).astype(BF16)
        w_lo = (w - w_hi.astype(F32)).astype(BF16)
        left = jnp.concatenate([w_hi, w_hi, w_lo], 0)
        right = jnp.concatenate([p_hi, p_lo, p_hi], 0)
        for m in range(0, 1024, 256):
            acc[m : m + 256, m:] -= over_rows(left[:, m : m + 256], right[:, m:])
        for m in range(256, 1024, 256):
            for n in range(0, m, 256):
                acc[m : m + 256, n : n + 256] = acc[n : n + 256, m : m + 256].T
        same = lax.broadcasted_iota(jnp.int32, (TILE, TILE), 0) == lax.broadcasted_iota(
            jnp.int32, (TILE, TILE), 1
        )
        for k in range(CLASSES):
            for m in range(CLASSES):
                for q in range(CHUNKS):
                    rows = k * TILE + q * PART
                    out[q, k, m % 4, m // 4] = acc[rows : rows + PART, m * TILE : (m + 1) * TILE]
            tile = acc[k * TILE : (k + 1) * TILE, k * TILE : (k + 1) * TILE]
            diag[k : k + 1, :] = jnp.sum(jnp.where(same, tile, 0.0), axis=0, keepdims=True)


def make_block(coupling, modes, flexibility, width, perm):
    steps = coupling.shape[1] // DEPTH
    count = modes.shape[1]

    def column(k, i, perm, width):
        return (0, i, perm[k])

    return pl.pallas_call(
        functools.partial(block_kernel, steps),
        grid_spec=pltpu.PrefetchScalarGridSpec(
            num_scalar_prefetch=2,
            grid=(steps,),
            in_specs=[
                pl.BlockSpec((1, DEPTH, TILE), functools.partial(column, k)) for k in range(CLASSES)
            ]
            + [
                pl.BlockSpec((1, count, DEPTH), lambda i, perm, width: (0, 0, i)),
                pl.BlockSpec((count, 1), lambda i, perm, width: (0, 0)),
            ],
            out_specs=[
                pl.BlockSpec((CHUNKS, 8, 4, 2, PART, TILE), lambda i, perm, width: (0,) * 6),
                pl.BlockSpec((CLASSES, TILE), lambda i, perm, width: (0, 0)),
            ],
            scratch_shapes=[
                pltpu.VMEM((DEPTH, 1024), BF16),
                pltpu.VMEM((1024, 1024), F32),
                pltpu.VMEM((count, 1024), F32),
            ],
        ),
        out_shape=[
            jax.ShapeDtypeStruct((CHUNKS, 8, 4, 2, PART, TILE), F32),
            jax.ShapeDtypeStruct((CLASSES, TILE), F32),
        ],
        compiler_params=pltpu.CompilerParams(vmem_limit_bytes=48 << 20),
        name="block",
    )(perm, width, *([coupling] * CLASSES), modes, flexibility.reshape(count, 1))


def exchange_kernel(cap, order, tiles, diag, ring_out, own_out, diag_out, *scratch):
    held, scratch = scratch[:CHUNKS], scratch[CHUNKS:]
    send, diag_held, diag_send, a_send, a_recv, b_send, b_recv, o_sem, d_sem = scratch
    row, col = lax.axis_index("row"), lax.axis_index("col")
    y, z = col // 4, col % 4
    mine = row * 4 + z

    def plane_peer(step):
        there = lax.rem(mine + step, PLANE)
        return there, (there // 4, y * 4 + lax.rem(there, 4))

    def ring_peer(step):
        return (row, lax.rem(y + step, RING) * 4 + z)

    barrier = pltpu.get_barrier_semaphore()

    def greet(step, carry):
        pl.semaphore_signal(barrier, inc=1, device_id=plane_peer(step)[1], device_id_type=MESH)
        return carry

    lax.fori_loop(1, PLANE, greet, 0)
    for step in range(1, RING):
        pl.semaphore_signal(barrier, inc=1, device_id=ring_peer(step), device_id_type=MESH)
    pl.semaphore_wait(barrier, PLANE - 1 + RING - 1)

    own_copies = []

    def local(src, dst, sem):
        copy = pltpu.make_async_copy(src, dst, sem)
        copy.start()
        return copy

    def send_diag(step, carry):
        pltpu.make_async_remote_copy(
            src_ref=diag,
            dst_ref=diag_held.at[mine],
            send_sem=d_sem.at[0],
            recv_sem=d_sem.at[1],
            device_id=plane_peer(step)[1],
            device_id_type=MESH,
        ).start()
        return carry

    lax.fori_loop(1, PLANE, send_diag, 0)
    own_diag = local(diag, diag_held.at[mine], d_sem.at[2])
    for q in range(CHUNKS):

        def send_tiles(step, carry, q=q):
            there, peer = plane_peer(step)
            pltpu.make_async_remote_copy(
                src_ref=tiles.at[q, there // 4, lax.rem(there, 4)],
                dst_ref=held[q].at[mine],
                send_sem=a_send.at[q],
                recv_sem=a_recv.at[q],
                device_id=peer,
                device_id_type=MESH,
            ).start()
            return carry

        lax.fori_loop(1, PLANE, send_tiles, 0)
        own_copies.append(local(tiles.at[q, row, z], held[q].at[mine], o_sem.at[0, q]))

    def whole(ref, sem):
        part = ref.at[pl.ds(0, PLANE - 1)]
        pltpu.make_async_copy(part, part, sem).wait()

    pending = []
    whole(diag_held, d_sem.at[1])
    own_diag.wait()

    def pick(i, carry):
        for parity in range(2):
            diag_send[parity, 0, pl.ds(i, 1), :] = diag_held[i, pl.ds(row, 1), :]
            diag_send[parity, 1, pl.ds(i, 1), :] = diag_held[i, pl.ds(4 * parity + z, 1), :]
        return carry

    lax.fori_loop(0, PLANE, pick, 0)
    here = local(diag_send.at[lax.rem(y, 2)], diag_out.at[0], d_sem.at[3])
    for step in range(1, RING):
        copy = pltpu.make_async_remote_copy(
            src_ref=diag_send.at[lax.rem(y + step, 2)],
            dst_ref=diag_out.at[step],
            send_sem=b_send.at[CHUNKS, step - 1],
            recv_sem=b_recv.at[CHUNKS, step - 1],
            device_id=ring_peer(step),
            device_id_type=MESH,
        )
        copy.start()
        pending.append(copy)
    for q in range(CHUNKS):
        whole(held[q], a_recv.at[q])
        own_copies[q].wait()
        for step in range(1, RING):
            parity = lax.rem(y + step, 2)

            def arrange(j, carry, q=q, step=step, parity=parity):
                send[q, step - 1, j] = held[q][order[step - 1, j], parity]
                return carry

            lax.fori_loop(0, cap, arrange, 0)
            copy = pltpu.make_async_remote_copy(
                src_ref=send.at[q, step - 1],
                dst_ref=ring_out.at[q, step - 1, pl.ds(0, cap)],
                send_sem=b_send.at[q, step - 1],
                recv_sem=b_recv.at[q, step - 1],
                device_id=ring_peer(step),
                device_id_type=MESH,
            )
            copy.start()
            pending.append(copy)
        own_copies[q] = local(held[q].at[:, lax.rem(y, 2)], own_out.at[q], o_sem.at[1, q])
    for copy in pending:
        copy.wait()
    for copy in own_copies:
        copy.wait()
    here.wait()
    whole(diag_held, d_sem.at[0])
    for q in range(CHUNKS):
        whole(held[q], a_send.at[q])


def exchange(cap, order, tiles, diag):
    dma = pltpu.SemaphoreType.DMA
    anywhere = pl.BlockSpec(memory_space=pl.ANY)
    return pl.pallas_call(
        functools.partial(exchange_kernel, cap),
        in_specs=[pl.BlockSpec(memory_space=pltpu.SMEM), anywhere, anywhere],
        out_specs=[anywhere] * 3,
        out_shape=[
            jax.ShapeDtypeStruct((CHUNKS, RING - 1, PLANE, PART, TILE), F32),
            jax.ShapeDtypeStruct((CHUNKS, PLANE, PART, TILE), F32),
            jax.ShapeDtypeStruct((RING, 2, PLANE, TILE), F32),
        ],
        scratch_shapes=[pltpu.VMEM((PLANE, 2, PART, TILE), F32)] * CHUNKS
        + [
            pltpu.VMEM((CHUNKS, RING - 1, cap, PART, TILE), F32),
            pltpu.VMEM((PLANE, CLASSES, TILE), F32),
            pltpu.VMEM((2, 2, PLANE, TILE), F32),
            dma((CHUNKS,)),
            dma((CHUNKS,)),
            dma((CHUNKS + 1, RING - 1)),
            dma((CHUNKS + 1, RING - 1)),
            dma((2, CHUNKS)),
            dma((4,)),
        ],
        compiler_params=pltpu.CompilerParams(
            collective_id=cap, has_side_effects=True, vmem_limit_bytes=40 << 20
        ),
        name="exchange",
    )(order, tiles, diag)


def assemble_kernel(count, place, ring, own, diag, row_hot, col_hot, out, row_scale, col_scale):
    chunk = pl.program_id(0)

    @pl.when(chunk == 0)
    def _():
        rows = lax.dot_general(
            diag[:, 0].reshape(RING * PLANE, TILE),
            row_hot[...],
            (((0,), (0,)), ((), ())),
            precision=HIGH,
            preferred_element_type=F32,
        )
        cols = jnp.dot(
            col_hot[...],
            diag[:, 1].reshape(RING * PLANE, TILE),
            precision=HIGH,
            preferred_element_type=F32,
        )
        row_scale[...] = 1.0 / jnp.sqrt(1.0 + jnp.abs(rows))
        col_scale[...] = 1.0 / jnp.sqrt(1.0 + jnp.abs(cols))

    out[...] = jnp.zeros_like(out)
    for d in range(RING):

        def add(j, carry, d=d):
            code = place[d, j]
            tile = own[0, code & 31] if d == 0 else ring[0, d - 1, j]
            across = pl.ds(pl.multiple_of((code >> 9) * TILE, TILE), TILE)
            out[(code >> 5) & 15, 0, :, across] += tile
            return carry

        lax.fori_loop(0, count[d], add, 0)
    inside = pl.ds(pl.multiple_of(chunk * PART, PART), PART)
    for g in range(ROW_TILES):
        for h in range(COL_TILES):
            scale = row_scale[inside, g : g + 1] * col_scale[h : h + 1, :]
            out[g, 0, :, h * TILE : (h + 1) * TILE] *= scale


def assemble(cap, count, place, ring, own, diag, row_hot, col_hot):
    return pl.pallas_call(
        assemble_kernel,
        grid_spec=pltpu.PrefetchScalarGridSpec(
            num_scalar_prefetch=2,
            grid=(CHUNKS,),
            in_specs=[
                pl.BlockSpec((1, RING - 1, cap, PART, TILE), lambda q, n, p: (q, 0, 0, 0, 0)),
                pl.BlockSpec((1, PLANE, PART, TILE), lambda q, n, p: (q, 0, 0, 0)),
                pl.BlockSpec((RING, 2, PLANE, TILE), lambda q, n, p: (0, 0, 0, 0)),
                pl.BlockSpec((RING * PLANE, 16), lambda q, n, p: (0, 0)),
                pl.BlockSpec((8, RING * PLANE), lambda q, n, p: (0, 0)),
            ],
            out_specs=pl.BlockSpec(
                (ROW_TILES, 1, PART, COL_TILES * TILE), lambda q, n, p: (0, q, 0, 0)
            ),
            scratch_shapes=[pltpu.VMEM((TILE, 16), F32), pltpu.VMEM((8, TILE), F32)],
        ),
        out_shape=jax.ShapeDtypeStruct((ROW_TILES, CHUNKS, PART, COL_TILES * TILE), F32),
        compiler_params=pltpu.CompilerParams(vmem_limit_bytes=40 << 20),
        name="assemble",
    )(count, place, ring, own, diag, row_hot, col_hot)


def sum_where(mask, values, axis):
    return jnp.sum(jnp.where(mask, values, 0), axis=axis)


def places(segments, row, col):
    y, z = col // 4, col % 4
    iota8 = jnp.arange(8, dtype=jnp.int32)
    slots = jnp.arange(PLANE, dtype=jnp.int32)
    steps = jnp.arange(RING, dtype=jnp.int32)
    in_class = (segments & 7)[:, :, None] == iota8
    by_class = sum_where(in_class, segments[:, :, None], 1)
    mine = jnp.arange(128, dtype=jnp.int32)[:, None] == row * 16 + col
    perm = sum_where(in_class & mine[:, :, None], iota8[None, :, None], (0, 1))
    planes = by_class.reshape(8, RING, 4, 8)
    ring = (y - steps) & 3
    from_plane = ring[:, None, None, None, None] == steps[None, None, :, None, None]
    held = sum_where(from_plane, planes[None], 2).reshape(RING, PLANE, 8)
    row_seg = sum_where(iota8 == row, held, 2)
    col_seg = sum_where(iota8 == (col & 7), held, 2)
    goes = (y + steps) & 3
    out_seg = sum_where(iota8 == (4 * (goes & 1) + z)[:, None, None], held[:1], 2)
    arrives = ((col_seg >> 3) & 1) == (col >> 3)
    leaves = ((out_seg >> 3) & 1) == (goes >> 1)[:, None]
    flags = jnp.stack([arrives, leaves])
    before = slots[:, None] > slots[None, :]
    rank = jnp.sum((flags[:, :, None, :] & before).astype(jnp.int32), axis=3)
    lands = flags[:, :, None, :] & (rank[:, :, None, :] == slots[:, None])
    codes = slots + 32 * (row_seg >> 3) + 512 * (col_seg >> 4)
    values = jnp.stack([codes, jnp.broadcast_to(slots, codes.shape)])
    table = sum_where(lands, values[:, :, None, :], 3)
    count = jnp.sum(arrives.astype(jnp.int32), axis=1)
    row_hot = (row_seg.reshape(-1)[:, None] >> 3) == jnp.arange(16, dtype=jnp.int32)
    col_place = jnp.where(arrives, col_seg >> 4, -1).reshape(-1)
    col_hot = col_place[None, :] == iota8[:, None]
    high = jnp.sum((planes >> 3) & 1, axis=(0, 2))
    held_by = jnp.stack([PLANE - high, high])
    goal = 2 * steps[:2, None, None] + (iota8 >> 2)
    need = jnp.max(jnp.where(goal == steps[:, None], 0, held_by))
    return perm, table[1, 1:], need, count, table[0], row_hot.astype(F32), col_hot.astype(F32)


def body(coupling, modes, flexibility, widths, segments):
    row, col = lax.axis_index("row"), lax.axis_index("col")
    perm, order, need, count, place, row_hot, col_hot = places(segments, row, col)
    tiles, diag = make_block(coupling, modes, flexibility[0], widths, perm)

    def within(cap):
        def run(order, tiles, diag, count, place, row_hot, col_hot):
            ring, own, diags = exchange(cap, order, tiles, diag)
            return assemble(cap, count, place, ring, own, diags, row_hot, col_hot)

        return run

    level = jnp.sum((need > jnp.array(CAPS[:-1])).astype(jnp.int32))
    out = lax.switch(
        level, [within(cap) for cap in CAPS], order, tiles, diag, count, place, row_hot, col_hot
    )
    return out.reshape(ROW_TILES * TILE, COL_TILES * TILE)


def solution(mesh):
    both = ("row", "col")
    return jax.shard_map(
        body,
        mesh=mesh,
        in_specs=(P(both, None, None), P(both, None, None), P(both, None), P(both), P()),
        out_specs=P("row", "col"),
        check_vma=False,
    )
```

```python
import functools

import jax
import jax.numpy as jnp
from jax import lax
from jax.experimental import pallas as pl
from jax.experimental.pallas import tpu as pltpu
from jax.sharding import PartitionSpec as P

TILE = 128
CHUNKS = 8
PART = TILE // CHUNKS
CLASSES = 8
PLANE = 32
RING = 4
ROW_TILES = 12
COL_TILES = 6
DEPTH = 1024
GROUP = 4
CAPS = (20, 22, 23, 24, 26, PLANE)
F32 = jnp.float32
BF16 = jnp.bfloat16
MESH = pl.DeviceIdType.MESH
HIGH = lax.Precision.HIGHEST


def over_rows(left, right):
    return lax.dot_general(left, right, (((0,), (0,)), ((), ())), preferred_element_type=F32)


def block_kernel(steps, perm, width, *refs):
    columns, (modes, weights, out, diag, masked, acc, proj) = refs[:CLASSES], refs[CLASSES:]
    step = pl.program_id(0)
    for k in range(CLASSES):
        lane = lax.broadcasted_iota(jnp.int32, (DEPTH, TILE), 1) + perm[k] * TILE
        masked[:, k * TILE : (k + 1) * TILE] = jnp.where(
            lane < width[0], columns[k][0], jnp.zeros((), BF16)
        )

    @pl.when(step == 0)
    def _():
        acc[...] = jnp.zeros_like(acc)
        proj[...] = jnp.zeros_like(proj)

    proj[...] += jnp.dot(modes[0], masked[...], preferred_element_type=F32)
    for m in range(0, 1024, 256):
        acc[m : m + 256, m:] += over_rows(masked[:, m : m + 256], masked[:, m:])

    @pl.when(step == steps - 1)
    def _():
        p = proj[...]
        count = p.shape[0]
        square = lax.broadcasted_iota(jnp.int32, (count, count), 0) == lax.broadcasted_iota(
            jnp.int32, (count, count), 1
        )
        w = p * jnp.sum(jnp.where(square, weights[...], 0.0), axis=1, keepdims=True)
        p_hi, w_hi = p.astype(BF16), w.astype(BF16)
        p_lo = (p - p_hi.astype(F32)).astype(BF16)
        w_lo = (w - w_hi.astype(F32)).astype(BF16)
        left = jnp.concatenate([w_hi, w_hi, w_lo], 0)
        right = jnp.concatenate([p_hi, p_lo, p_hi], 0)
        for m in range(0, 1024, 256):
            acc[m : m + 256, m:] -= over_rows(left[:, m : m + 256], right[:, m:])
        for m in range(256, 1024, 256):
            for n in range(0, m, 256):
                acc[m : m + 256, n : n + 256] = acc[n : n + 256, m : m + 256].T
        same = lax.broadcasted_iota(jnp.int32, (TILE, TILE), 0) == lax.broadcasted_iota(
            jnp.int32, (TILE, TILE), 1
        )
        for k in range(CLASSES):
            for m in range(CLASSES):
                for q in range(CHUNKS):
                    rows = k * TILE + q * PART
                    out[q, k, m % 4, m // 4] = acc[rows : rows + PART, m * TILE : (m + 1) * TILE]
            tile = acc[k * TILE : (k + 1) * TILE, k * TILE : (k + 1) * TILE]
            diag[k : k + 1, :] = jnp.sum(jnp.where(same, tile, 0.0), axis=0, keepdims=True)


def make_block(coupling, modes, flexibility, width, perm):
    steps = coupling.shape[1] // DEPTH
    count = modes.shape[1]

    def column(k, i, perm, width):
        return (0, i, perm[k])

    return pl.pallas_call(
        functools.partial(block_kernel, steps),
        grid_spec=pltpu.PrefetchScalarGridSpec(
            num_scalar_prefetch=2,
            grid=(steps,),
            in_specs=[
                pl.BlockSpec((1, DEPTH, TILE), functools.partial(column, k)) for k in range(CLASSES)
            ]
            + [
                pl.BlockSpec((1, count, DEPTH), lambda i, perm, width: (0, 0, i)),
                pl.BlockSpec((1, count), lambda i, perm, width: (0, 0)),
            ],
            out_specs=[
                pl.BlockSpec((CHUNKS, 8, 4, 2, PART, TILE), lambda i, perm, width: (0,) * 6),
                pl.BlockSpec((CLASSES, TILE), lambda i, perm, width: (0, 0)),
            ],
            scratch_shapes=[
                pltpu.VMEM((DEPTH, 1024), BF16),
                pltpu.VMEM((1024, 1024), F32),
                pltpu.VMEM((count, 1024), F32),
            ],
        ),
        out_shape=[
            jax.ShapeDtypeStruct((CHUNKS, 8, 4, 2, PART, TILE), F32),
            jax.ShapeDtypeStruct((CLASSES, TILE), F32),
        ],
        compiler_params=pltpu.CompilerParams(vmem_limit_bytes=48 << 20),
        name="block",
    )(perm, width, *([coupling] * CLASSES), modes, flexibility)


def exchange_kernel(cap, order, tiles, diag, ring_out, own_out, diag_out, *scratch):
    held, scratch = scratch[:CHUNKS], scratch[CHUNKS:]
    send, diag_held, diag_send, a_send, a_recv, b_send, b_recv, o_sem, d_sem = scratch
    row, col = lax.axis_index("row"), lax.axis_index("col")
    y, z = col // 4, col % 4
    mine = row * 4 + z

    def plane_peer(step):
        there = lax.rem(mine + step, PLANE)
        return there, (there // 4, y * 4 + lax.rem(there, 4))

    def ring_peer(step):
        return (row, lax.rem(y + step, RING) * 4 + z)

    barrier = pltpu.get_barrier_semaphore()

    def greet(step, carry):
        pl.semaphore_signal(barrier, inc=1, device_id=plane_peer(step)[1], device_id_type=MESH)
        return carry

    lax.fori_loop(1, PLANE, greet, 0)
    for step in range(1, RING):
        pl.semaphore_signal(barrier, inc=1, device_id=ring_peer(step), device_id_type=MESH)
    pl.semaphore_wait(barrier, PLANE - 1 + RING - 1)

    own_copies = []

    def local(src, dst, sem):
        copy = pltpu.make_async_copy(src, dst, sem)
        copy.start()
        return copy

    def send_diag(step, carry):
        pltpu.make_async_remote_copy(
            src_ref=diag,
            dst_ref=diag_held.at[mine],
            send_sem=d_sem.at[0],
            recv_sem=d_sem.at[1],
            device_id=plane_peer(step)[1],
            device_id_type=MESH,
        ).start()
        return carry

    lax.fori_loop(1, PLANE, send_diag, 0)
    own_diag = local(diag, diag_held.at[mine], d_sem.at[2])
    for q in range(CHUNKS):

        def send_tiles(step, carry, q=q):
            there, peer = plane_peer(step)
            pltpu.make_async_remote_copy(
                src_ref=tiles.at[q, there // 4, lax.rem(there, 4)],
                dst_ref=held[q].at[mine],
                send_sem=a_send.at[q],
                recv_sem=a_recv.at[q],
                device_id=peer,
                device_id_type=MESH,
            ).start()
            return carry

        lax.fori_loop(1, PLANE, send_tiles, 0)
        own_copies.append(local(tiles.at[q, row, z], held[q].at[mine], o_sem.at[0, q]))

    def whole(ref, sem):
        part = ref.at[pl.ds(0, PLANE - 1)]
        pltpu.make_async_copy(part, part, sem).wait()

    pending = []
    whole(diag_held, d_sem.at[1])
    own_diag.wait()

    def pick(i, carry):
        for parity in range(2):
            diag_send[parity, 0, pl.ds(i, 1), :] = diag_held[i, pl.ds(row, 1), :]
            diag_send[parity, 1, pl.ds(i, 1), :] = diag_held[i, pl.ds(4 * parity + z, 1), :]
        return carry

    lax.fori_loop(0, PLANE, pick, 0)
    here = local(diag_send.at[lax.rem(y, 2)], diag_out.at[0], d_sem.at[3])
    for step in range(1, RING):
        copy = pltpu.make_async_remote_copy(
            src_ref=diag_send.at[lax.rem(y + step, 2)],
            dst_ref=diag_out.at[step],
            send_sem=b_send.at[CHUNKS, step - 1],
            recv_sem=b_recv.at[CHUNKS, step - 1],
            device_id=ring_peer(step),
            device_id_type=MESH,
        )
        copy.start()
        pending.append(copy)
    for q in range(CHUNKS):
        whole(held[q], a_recv.at[q])
        own_copies[q].wait()
        for step in range(1, RING):
            parity = lax.rem(y + step, 2)

            def arrange(j, carry, q=q, step=step, parity=parity):
                send[q, step - 1, j] = held[q][order[step - 1, j], parity]
                return carry

            lax.fori_loop(0, cap, arrange, 0)
            copy = pltpu.make_async_remote_copy(
                src_ref=send.at[q, step - 1],
                dst_ref=ring_out.at[q, step - 1, pl.ds(0, cap)],
                send_sem=b_send.at[q, step - 1],
                recv_sem=b_recv.at[q, step - 1],
                device_id=ring_peer(step),
                device_id_type=MESH,
            )
            copy.start()
            pending.append(copy)
        own_copies[q] = local(held[q].at[:, lax.rem(y, 2)], own_out.at[q], o_sem.at[1, q])
    for copy in pending:
        copy.wait()
    for copy in own_copies:
        copy.wait()
    here.wait()
    whole(diag_held, d_sem.at[0])
    for q in range(CHUNKS):
        whole(held[q], a_send.at[q])


def exchange(cap, order, tiles, diag):
    dma = pltpu.SemaphoreType.DMA
    anywhere = pl.BlockSpec(memory_space=pl.ANY)
    return pl.pallas_call(
        functools.partial(exchange_kernel, cap),
        in_specs=[pl.BlockSpec(memory_space=pltpu.SMEM), anywhere, anywhere],
        out_specs=[anywhere] * 3,
        out_shape=[
            jax.ShapeDtypeStruct((CHUNKS, RING - 1, PLANE, PART, TILE), F32),
            jax.ShapeDtypeStruct((CHUNKS, PLANE, PART, TILE), F32),
            jax.ShapeDtypeStruct((RING, 2, PLANE, TILE), F32),
        ],
        scratch_shapes=[pltpu.VMEM((PLANE, 2, PART, TILE), F32)] * CHUNKS
        + [
            pltpu.VMEM((CHUNKS, RING - 1, cap, PART, TILE), F32),
            pltpu.VMEM((PLANE, CLASSES, TILE), F32),
            pltpu.VMEM((2, 2, PLANE, TILE), F32),
            dma((CHUNKS,)),
            dma((CHUNKS,)),
            dma((CHUNKS + 1, RING - 1)),
            dma((CHUNKS + 1, RING - 1)),
            dma((2, CHUNKS)),
            dma((4,)),
        ],
        compiler_params=pltpu.CompilerParams(
            collective_id=cap, has_side_effects=True, vmem_limit_bytes=40 << 20
        ),
        name="exchange",
    )(order, tiles, diag)


def assemble_kernel(count, place, ring, own, diag, row_hot, col_hot, out, row_scale, col_scale):
    chunk = pl.program_id(0)

    @pl.when(chunk == 0)
    def _():
        rows = lax.dot_general(
            diag[:, 0].reshape(RING * PLANE, TILE),
            row_hot[...],
            (((0,), (0,)), ((), ())),
            precision=HIGH,
            preferred_element_type=F32,
        )
        cols = jnp.dot(
            col_hot[...],
            diag[:, 1].reshape(RING * PLANE, TILE),
            precision=HIGH,
            preferred_element_type=F32,
        )
        row_scale[...] = 1.0 / jnp.sqrt(1.0 + jnp.abs(rows))
        col_scale[...] = 1.0 / jnp.sqrt(1.0 + jnp.abs(cols))

    out[...] = jnp.zeros_like(out)
    for d in range(RING):

        def add(j, carry, d=d):
            code = place[d, j]
            tile = own[:, code & 31] if d == 0 else ring[:, d - 1, j]
            across = pl.ds(pl.multiple_of((code >> 9) * TILE, TILE), TILE)
            out[(code >> 5) & 15, :, :, across] += tile
            return carry

        lax.fori_loop(0, count[d], add, 0)
    for part in range(GROUP):
        inside = pl.ds(pl.multiple_of((chunk * GROUP + part) * PART, PART), PART)
        for g in range(ROW_TILES):
            for h in range(COL_TILES):
                scale = row_scale[inside, g : g + 1] * col_scale[h : h + 1, :]
                out[g, part, :, h * TILE : (h + 1) * TILE] *= scale


def assemble(count, place, ring, own, diag, row_hot, col_hot):
    return pl.pallas_call(
        assemble_kernel,
        grid_spec=pltpu.PrefetchScalarGridSpec(
            num_scalar_prefetch=2,
            grid=(CHUNKS // GROUP,),
            in_specs=[
                pl.BlockSpec((GROUP, RING - 1, PLANE, PART, TILE), lambda q, n, p: (q, 0, 0, 0, 0)),
                pl.BlockSpec((GROUP, PLANE, PART, TILE), lambda q, n, p: (q, 0, 0, 0)),
                pl.BlockSpec((RING, 2, PLANE, TILE), lambda q, n, p: (0, 0, 0, 0)),
                pl.BlockSpec((RING * PLANE, 16), lambda q, n, p: (0, 0)),
                pl.BlockSpec((8, RING * PLANE), lambda q, n, p: (0, 0)),
            ],
            out_specs=pl.BlockSpec(
                (ROW_TILES, GROUP, PART, COL_TILES * TILE), lambda q, n, p: (0, q, 0, 0)
            ),
            scratch_shapes=[pltpu.VMEM((TILE, 16), F32), pltpu.VMEM((8, TILE), F32)],
        ),
        out_shape=jax.ShapeDtypeStruct((ROW_TILES, CHUNKS, PART, COL_TILES * TILE), F32),
        compiler_params=pltpu.CompilerParams(vmem_limit_bytes=40 << 20),
        name="assemble",
    )(count, place, ring, own, diag, row_hot, col_hot)


def sum_where(mask, values, axis):
    return jnp.sum(jnp.where(mask, values, 0), axis=axis)


def places(segments, row, col):
    y, z = col // 4, col % 4
    iota8 = jnp.arange(8, dtype=jnp.int32)
    slots = jnp.arange(PLANE, dtype=jnp.int32)
    steps = jnp.arange(RING, dtype=jnp.int32)
    in_class = (segments & 7)[:, :, None] == iota8
    by_class = sum_where(in_class, segments[:, :, None], 1)
    mine = jnp.arange(128, dtype=jnp.int32)[:, None] == row * 16 + col
    perm = sum_where(in_class & mine[:, :, None], iota8[None, :, None], (0, 1))
    planes = by_class.reshape(8, RING, 4, 8)
    ring = (y - steps) & 3
    from_plane = ring[:, None, None, None, None] == steps[None, None, :, None, None]
    held = sum_where(from_plane, planes[None], 2).reshape(RING, PLANE, 8)
    row_seg = sum_where(iota8 == row, held, 2)
    col_seg = sum_where(iota8 == (col & 7), held, 2)
    goes = (y + steps) & 3
    out_seg = sum_where(iota8 == (4 * (goes & 1) + z)[:, None, None], held[:1], 2)
    arrives = ((col_seg >> 3) & 1) == (col >> 3)
    leaves = ((out_seg >> 3) & 1) == (goes >> 1)[:, None]
    flags = jnp.stack([arrives, leaves])
    before = slots[:, None] > slots[None, :]
    rank = jnp.sum((flags[:, :, None, :] & before).astype(jnp.int32), axis=3)
    lands = flags[:, :, None, :] & (rank[:, :, None, :] == slots[:, None])
    codes = slots + 32 * (row_seg >> 3) + 512 * (col_seg >> 4)
    values = jnp.stack([codes, jnp.broadcast_to(slots, codes.shape)])
    table = sum_where(lands, values[:, :, None, :], 3)
    count = jnp.sum(arrives.astype(jnp.int32), axis=1)
    row_hot = (row_seg.reshape(-1)[:, None] >> 3) == jnp.arange(16, dtype=jnp.int32)
    col_place = jnp.where(arrives, col_seg >> 4, -1).reshape(-1)
    col_hot = col_place[None, :] == iota8[:, None]
    high = jnp.sum((planes >> 3) & 1, axis=(0, 2))
    held_by = jnp.stack([PLANE - high, high])
    goal = 2 * steps[:2, None, None] + (iota8 >> 2)
    need = jnp.max(jnp.where(goal == steps[:, None], 0, held_by))
    return perm, table[1, 1:], need, count, table[0], row_hot.astype(F32), col_hot.astype(F32)


def body(coupling, modes, flexibility, widths, segments):
    row, col = lax.axis_index("row"), lax.axis_index("col")
    perm, order, need, count, place, row_hot, col_hot = places(segments, row, col)
    tiles, diag = make_block(coupling, modes, flexibility, widths, perm)

    level = jnp.sum((need > jnp.array(CAPS[:-1])).astype(jnp.int32))
    ring, own, diags = lax.switch(
        level, [functools.partial(exchange, cap) for cap in CAPS], order, tiles, diag
    )
    out = assemble(count, place, ring, own, diags, row_hot, col_hot)
    return out.reshape(ROW_TILES * TILE, COL_TILES * TILE)


def solution(mesh):
    both = ("row", "col")
    return jax.shard_map(
        body,
        mesh=mesh,
        in_specs=(P(both, None, None), P(both, None, None), P(both, None), P(both), P()),
        out_specs=P("row", "col"),
        check_vma=False,
    )
```

```python
import functools

import jax
import jax.numpy as jnp
from jax import lax
from jax.experimental import pallas as pl
from jax.experimental.pallas import tpu as pltpu
from jax.sharding import PartitionSpec as P

TILE = 128
PARTS = (16,) * 8
AHEAD = 2
CLASSES = 8
PLANE = 32
RING = 4
ROW_TILES = 12
COL_TILES = 6
DEPTH = 1024
STEPS = 4
SPAN = 64
CAPS = (17, 18, 19, 20, 21, 23, PLANE)
F32 = jnp.float32
BF16 = jnp.bfloat16
MESH = pl.DeviceIdType.MESH
HIGH = lax.Precision.HIGHEST


def over_rows(left, right):
    return lax.dot_general(left, right, (((0,), (0,)), ((), ())), preferred_element_type=F32)


def block_kernel(segments, width, coupling, modes, weights, wide, out, diag, all_wide, *scratch):
    raw, mode_rows, tiles, acc, proj, m_sem, p_sem, w_sem, r_sem, t_sem = scratch
    row, col = lax.axis_index("row"), lax.axis_index("col")
    y, z = col // 4, col % 4
    mine = row * 4 + z

    def plane_peer(step):
        there = lax.rem(mine + step, PLANE)
        return (there // 4, y * 4 + lax.rem(there, 4))

    def ring_peer(step):
        return (row, lax.rem(y + step, RING) * 4 + z)

    def load(k):
        rows = pl.ds(k * DEPTH, DEPTH)
        return pltpu.make_async_copy(coupling.at[0, rows], raw.at[k], m_sem.at[k])

    mode_copy = pltpu.make_async_copy(modes.at[0], mode_rows, p_sem)
    load(0).start()
    mode_copy.start()
    for k in range(1, STEPS):
        load(k).start()
    barrier = pltpu.get_barrier_semaphore()

    def greet(step, carry):
        pl.semaphore_signal(barrier, inc=1, device_id=plane_peer(step), device_id_type=MESH)
        return carry

    lax.fori_loop(1, PLANE, greet, 0)
    for step in range(1, RING):
        pl.semaphore_signal(barrier, inc=1, device_id=ring_peer(step), device_id_type=MESH)
    acc[...] = jnp.zeros_like(acc)
    proj[...] = jnp.zeros_like(proj)
    here = pltpu.make_async_copy(wide, all_wide.at[y, mine], w_sem.at[2])

    def pass_on(step):
        return pltpu.make_async_remote_copy(
            src_ref=all_wide.at[y],
            dst_ref=all_wide.at[y],
            send_sem=r_sem.at[0, step - 1],
            recv_sem=r_sem.at[1, step - 1],
            device_id=ring_peer(step),
            device_id_type=MESH,
        )

    mode_copy.wait()

    def multiply(k, carry):
        load(k).wait()

        @pl.when(k == 1)
        def _():
            pl.semaphore_wait(barrier, PLANE - 1 + RING - 1)

            def tell(step, carry):
                pltpu.make_async_remote_copy(
                    src_ref=wide,
                    dst_ref=all_wide.at[y, mine],
                    send_sem=w_sem.at[0],
                    recv_sem=w_sem.at[1],
                    device_id=plane_peer(step),
                    device_id_type=MESH,
                ).start()
                return carry

            lax.fori_loop(1, PLANE, tell, 0)
            here.start()

        @pl.when(k == STEPS - 1)
        def _():
            others = all_wide.at[y, pl.ds(0, PLANE - 1)]
            pltpu.make_async_copy(others, others, w_sem.at[1]).wait()
            pltpu.make_async_copy(others, others, w_sem.at[0]).wait()
            here.wait()
            for step in range(1, RING):
                pass_on(step).start()

        cols = pl.ds(pl.multiple_of(k * DEPTH, DEPTH), DEPTH)
        proj[...] += jnp.dot(mode_rows[:, cols], raw[k], preferred_element_type=F32)
        for m in range(0, CLASSES, 2):
            part = over_rows(raw[k, :, m * TILE : (m + 2) * TILE], raw[k, :, m * TILE :])
            for i in range(2):
                for n in range(m, CLASSES):
                    inside = part[i * TILE : (i + 1) * TILE, (n - m) * TILE : (n - m + 1) * TILE]
                    acc[m + i, n] += inside
        return carry

    lax.fori_loop(0, STEPS, multiply, 0)
    p = proj[...]
    count = p.shape[0]
    square = lax.broadcasted_iota(jnp.int32, (count, count), 0) == lax.broadcasted_iota(
        jnp.int32, (count, count), 1
    )
    w = p * jnp.sum(jnp.where(square, weights[...], 0.0), axis=1, keepdims=True)
    p_hi, w_hi = p.astype(BF16), w.astype(BF16)
    p_lo = (p - p_hi.astype(F32)).astype(BF16)
    w_lo = (w - w_hi.astype(F32)).astype(BF16)
    left = jnp.concatenate([w_hi, w_hi, w_lo], 0)
    right = jnp.concatenate([p_hi, p_lo, p_hi], 0)
    for m in range(0, CLASSES, 2):
        part = over_rows(left[:, m * TILE : (m + 2) * TILE], right[:, m * TILE :])
        for i in range(2):
            for n in range(m, CLASSES):
                inside = part[i * TILE : (i + 1) * TILE, (n - m) * TILE : (n - m + 1) * TILE]
                tile = acc[m + i, n] - inside
                acc[m + i, n] = tile
                if n > m + 1:
                    acc[n, m + i] = tile.T
    perm = []
    for k in range(CLASSES):
        place = jnp.int32(0)
        for j in range(1, CLASSES):
            fits = (segments[row * 16 + col, j] & 7) == k
            place = jnp.where(fits, jnp.int32(j), place)
        perm.append(place)
    down = lax.broadcasted_iota(jnp.int32, (TILE, TILE), 0)
    across = lax.broadcasted_iota(jnp.int32, (TILE, TILE), 1)
    copies = []
    for k in range(CLASSES):
        above = down < width[0] - perm[k] * TILE
        for m in range(CLASSES):
            inside = above & (across < width[0] - perm[m] * TILE)
            tile = jnp.where(inside, acc[perm[k], perm[m]], 0.0)
            tiles[k, m % 4, m // 4] = tile
            if k == m:
                diag[k : k + 1, :] = jnp.sum(
                    jnp.where(down == across, tile, 0.0), axis=0, keepdims=True
                )
        copy = pltpu.make_async_copy(tiles.at[k], out.at[k], t_sem.at[k])
        copy.start()
        copies.append(copy)
    for step in range(1, RING):
        pass_on(step).wait()
    for copy in copies:
        copy.wait()


def make_block(coupling, modes, flexibility, width, segments):
    count = modes.shape[1]
    dma = pltpu.SemaphoreType.DMA
    scalars = pl.BlockSpec(memory_space=pltpu.SMEM)
    far, vectors = pl.BlockSpec(memory_space=pltpu.HBM), pl.BlockSpec(memory_space=pltpu.VMEM)
    wide = jnp.broadcast_to(width.astype(F32)[:, None], (1, TILE))
    return pl.pallas_call(
        block_kernel,
        in_specs=[scalars, scalars, far, far, vectors, vectors],
        out_specs=[pl.BlockSpec(memory_space=pl.ANY), vectors, vectors],
        out_shape=[
            jax.ShapeDtypeStruct((8, 4, 2, TILE, TILE), F32),
            jax.ShapeDtypeStruct((CLASSES, TILE), F32),
            jax.ShapeDtypeStruct((RING, PLANE, 1, TILE), F32),
        ],
        scratch_shapes=[
            pltpu.VMEM((STEPS, DEPTH, 1024), BF16),
            pltpu.VMEM((count, 4096), BF16),
            pltpu.VMEM((8, 4, 2, TILE, TILE), F32),
            pltpu.VMEM((CLASSES, CLASSES, TILE, TILE), F32),
            pltpu.VMEM((count, 1024), F32),
            dma((STEPS,)),
            dma,
            dma((3,)),
            dma((2, RING - 1)),
            dma((CLASSES,)),
        ],
        compiler_params=pltpu.CompilerParams(
            collective_id=1, has_side_effects=True, vmem_limit_bytes=60 << 20
        ),
        name="block",
    )(segments, width, coupling, modes, flexibility, wide)


def exchange_kernel(cap, table, tiles, diag, ring_out, own_out, diag_out, *scratch):
    chunks = len(PARTS)
    held, send, scratch = scratch[:chunks], scratch[chunks : 2 * chunks], scratch[2 * chunks :]
    spans = [pl.ds(sum(PARTS[:q]), PARTS[q]) for q in range(chunks)]
    diag_held, diag_send, a_send, a_recv, b_send, b_recv, o_sem, d_sem = scratch
    row, col = lax.axis_index("row"), lax.axis_index("col")
    y, z = col // 4, col % 4
    mine = row * 4 + z

    def plane_peer(step):
        there = lax.rem(mine + step, PLANE)
        return there, (there // 4, y * 4 + lax.rem(there, 4))

    def ring_peer(step):
        return (row, lax.rem(y + step, RING) * 4 + z)

    barrier = pltpu.get_barrier_semaphore()

    def greet(step, carry):
        pl.semaphore_signal(barrier, inc=1, device_id=plane_peer(step)[1], device_id_type=MESH)
        return carry

    lax.fori_loop(1, PLANE, greet, 0)
    for step in range(1, RING):
        pl.semaphore_signal(barrier, inc=1, device_id=ring_peer(step), device_id_type=MESH)
    pl.semaphore_wait(barrier, PLANE - 1 + RING - 1)

    own_copies, kept = [None] * chunks, []

    def local(src, dst, sem):
        copy = pltpu.make_async_copy(src, dst, sem)
        copy.start()
        return copy

    def send_diag(step, carry):
        pltpu.make_async_remote_copy(
            src_ref=diag,
            dst_ref=diag_held.at[mine],
            send_sem=d_sem.at[0],
            recv_sem=d_sem.at[1],
            device_id=plane_peer(step)[1],
            device_id_type=MESH,
        ).start()
        return carry

    def start_plane(q):
        def send_tiles(step, carry):
            there, peer = plane_peer(step)
            pltpu.make_async_remote_copy(
                src_ref=tiles.at[there // 4, lax.rem(there, 4), :, spans[q]],
                dst_ref=held[q].at[mine],
                send_sem=a_send.at[q],
                recv_sem=a_recv.at[q],
                device_id=peer,
                device_id_type=MESH,
            ).start()
            return carry

        lax.fori_loop(1, PLANE, send_tiles, 0)
        own_copies[q] = local(tiles.at[row, z, :, spans[q]], held[q].at[mine], o_sem.at[0, q])

    def whole(ref, sem):
        part = ref.at[pl.ds(0, PLANE - 1)]
        pltpu.make_async_copy(part, part, sem).wait()

    pending = []
    for q in range(AHEAD):
        start_plane(q)
    for q in range(chunks):
        whole(held[q], a_recv.at[q])
        own_copies[q].wait()
        for step in range(1, RING):
            parity = lax.rem(y + step, 2)

            def arrange(j, carry, q=q, step=step, parity=parity):
                send[q][step - 1, j] = held[q][table[3 + step, j], parity]
                return carry

            lax.fori_loop(0, cap, arrange, 0)
            copy = pltpu.make_async_remote_copy(
                src_ref=send[q].at[step - 1],
                dst_ref=ring_out.at[step - 1, pl.ds(0, cap), spans[q]],
                send_sem=b_send.at[q, step - 1],
                recv_sem=b_recv.at[q, step - 1],
                device_id=ring_peer(step),
                device_id_type=MESH,
            )
            copy.start()
            pending.append(copy)
        kept.append(local(held[q].at[:, lax.rem(y, 2)], own_out.at[:, spans[q]], o_sem.at[1, q]))
        if q + AHEAD < chunks:
            start_plane(q + AHEAD)
        if q == 1:
            own_diag = local(diag, diag_held.at[mine], d_sem.at[2])
            lax.fori_loop(1, PLANE, send_diag, 0)
        if q == 4:
            whole(diag_held, d_sem.at[1])
            own_diag.wait()

            def pick(i, carry):
                for parity in range(2):
                    diag_send[parity, 0, pl.ds(i, 1), :] = diag_held[i, pl.ds(row, 1), :]
                    diag_send[parity, 1, pl.ds(i, 1), :] = diag_held[i, pl.ds(4 * parity + z, 1), :]
                return carry

            lax.fori_loop(0, PLANE, pick, 0)
            here = local(diag_send.at[lax.rem(y, 2)], diag_out.at[0], d_sem.at[3])
            for step in range(1, RING):
                copy = pltpu.make_async_remote_copy(
                    src_ref=diag_send.at[lax.rem(y + step, 2)],
                    dst_ref=diag_out.at[step],
                    send_sem=b_send.at[chunks, step - 1],
                    recv_sem=b_recv.at[chunks, step - 1],
                    device_id=ring_peer(step),
                    device_id_type=MESH,
                )
                copy.start()
                pending.append(copy)
    for copy in pending:
        copy.wait()
    for copy in kept:
        copy.wait()
    here.wait()
    whole(diag_held, d_sem.at[0])
    for q in range(chunks):
        whole(held[q], a_send.at[q])


def exchange(cap, table, tiles, diag):
    dma = pltpu.SemaphoreType.DMA
    anywhere = pl.BlockSpec(memory_space=pl.ANY)
    return pl.pallas_call(
        functools.partial(exchange_kernel, cap),
        in_specs=[pl.BlockSpec(memory_space=pltpu.SMEM), anywhere, anywhere],
        out_specs=[anywhere] * 3,
        out_shape=[
            jax.ShapeDtypeStruct((RING - 1, PLANE, TILE, TILE), F32),
            jax.ShapeDtypeStruct((PLANE, TILE, TILE), F32),
            jax.ShapeDtypeStruct((RING, 2, PLANE, TILE), F32),
        ],
        scratch_shapes=[pltpu.VMEM((PLANE, 2, part, TILE), F32) for part in PARTS]
        + [pltpu.VMEM((RING - 1, cap, part, TILE), F32) for part in PARTS]
        + [
            pltpu.VMEM((PLANE, CLASSES, TILE), F32),
            pltpu.VMEM((2, 2, PLANE, TILE), F32),
            dma((len(PARTS),)),
            dma((len(PARTS),)),
            dma((len(PARTS) + 1, RING - 1)),
            dma((len(PARTS) + 1, RING - 1)),
            dma((2, len(PARTS))),
            dma((4,)),
        ],
        compiler_params=pltpu.CompilerParams(
            collective_id=cap + 1, has_side_effects=True, vmem_limit_bytes=40 << 20
        ),
        name="exchange",
    )(table, tiles, diag)


def exactly(left, right):
    return lax.dot_general(
        left, right, (((0,), (0,)), ((), ())), precision=HIGH, preferred_element_type=F32
    )


def assemble_kernel(table, ring, own, diag, row_hot, col_hot, out, row_scale, col_scale, acc, sem):
    rows = exactly(diag[:, 0].reshape(RING * PLANE, TILE), row_hot[...])
    cols = exactly(col_hot[...], diag[:, 1].reshape(RING * PLANE, TILE))[:8]
    row_scale[...] = 1.0 / jnp.sqrt(1.0 + jnp.abs(rows))
    col_scale[...] = 1.0 / jnp.sqrt(1.0 + jnp.abs(cols))
    copies = []
    for first in range(0, TILE, SPAN):
        span = slice(first, first + SPAN)
        acc[:, span] = jnp.zeros((ROW_TILES, SPAN, COL_TILES * TILE), F32)
        for d in range(RING):

            def add(j, carry, d=d, span=span):
                code = table[d, j]
                tile = own[code & 31, span] if d == 0 else ring[d - 1, j, span]
                across = pl.ds(pl.multiple_of((code >> 9) * TILE, TILE), TILE)
                acc[(code >> 5) & 15, span, across] += tile
                return carry

            lax.fori_loop(0, table[8 + d, 0], add, 0)
        for g in range(ROW_TILES):
            down = jnp.broadcast_to(row_scale[span, g : g + 1], (SPAN, TILE))
            for h in range(COL_TILES):
                acc[g, span, h * TILE : (h + 1) * TILE] *= down * col_scale[h : h + 1, :]
        copy = pltpu.make_async_copy(acc.at[:, span], out.at[:, span], sem.at[first // SPAN])
        copy.start()
        copies.append(copy)
    for copy in copies:
        copy.wait()


def assemble(table, ring, own, diag, row_hot, col_hot):
    scalars, vectors = pl.BlockSpec(memory_space=pltpu.SMEM), pl.BlockSpec(memory_space=pltpu.VMEM)
    shape = (ROW_TILES, TILE, COL_TILES * TILE)
    return pl.pallas_call(
        assemble_kernel,
        in_specs=[scalars] + [vectors] * 5,
        out_specs=pl.BlockSpec(memory_space=pl.ANY),
        out_shape=jax.ShapeDtypeStruct(shape, F32),
        scratch_shapes=[
            pltpu.VMEM((TILE, TILE), F32),
            pltpu.VMEM((8, TILE), F32),
            pltpu.VMEM(shape, F32),
            pltpu.SemaphoreType.DMA((TILE // SPAN,)),
        ],
        compiler_params=pltpu.CompilerParams(vmem_limit_bytes=24 << 20),
        name="assemble",
    )(table, ring, own, diag, row_hot, col_hot)


def places_kernel(segments, all_wide, table, row_hot, col_hot, plane, tags):
    row, col = lax.axis_index("row"), lax.axis_index("col")
    y, z = col // 4, col % 4
    lane = lax.broadcasted_iota(jnp.int32, (PLANE, TILE), 1)
    slot = lax.broadcasted_iota(jnp.int32, (PLANE, TILE), 0)
    lane8 = lax.broadcasted_iota(jnp.int32, (PLANE, CLASSES), 1)
    need = jnp.zeros((CLASSES, TILE), F32)
    half = lax.broadcasted_iota(jnp.int32, (CLASSES, TILE), 0) >> 2
    for p in range(RING):
        for k in range(CLASSES):
            first = 16 * k + 4 * p
            plane[p, 4 * k : 4 * k + 4, :] = segments[first : first + 4, :]
        numbers = plane[p]
        width = all_wide[p, :, 0, :].astype(jnp.int32)
        tag = jnp.zeros((PLANE, TILE), jnp.int32)
        for k in range(CLASSES):
            found = jnp.where((numbers & 7) == k, numbers + 128 * lane8, 0)
            found = jnp.broadcast_to(jnp.sum(found, axis=1, keepdims=True), (PLANE, TILE))
            used = jnp.where((found >> 7) * TILE < width, 128, 0)
            tag = jnp.where(lane == k, (found & 127) + used, tag)
        tags[p] = tag
        filled = (tag >> 7).astype(F32)
        high = ((tag >> 3) & 1).astype(F32)
        for h, part in ((0, filled * (1.0 - high)), (1, filled * high)):
            held = over_rows(part, filled)[:CLASSES]
            need = jnp.maximum(need, jnp.where(2 * h + half == p, 0.0, held))

    def column(values, index):
        picked = jnp.sum(jnp.where(lane == index, values, 0), axis=1, keepdims=True)
        return jnp.broadcast_to(picked, (PLANE, TILE))

    earlier = lax.broadcasted_iota(jnp.int32, (PLANE, PLANE), 0) > lax.broadcasted_iota(
        jnp.int32, (PLANE, PLANE), 1
    )
    earlier = jnp.where(earlier, 1.0, 0.0).astype(F32)

    def listed(flag, values):
        rank = jnp.dot(earlier, jnp.where(flag, 1.0, 0.0), preferred_element_type=F32)
        lands = flag & (rank.astype(jnp.int32) == lane)
        return jnp.sum(jnp.where(lands, values, 0), axis=0, keepdims=True)

    table[...] = jnp.zeros((16, TILE), jnp.int32)
    here = tags[y]
    mine = column(here, row)
    for d in range(RING):
        tag = tags[(y - d) & 3]
        down, across = column(tag, row), column(tag, col & 7)
        owned = ((across >> 3) & 1) == (col >> 3)
        arrives = owned & (down > 127) & (across > 127)
        code = slot + 32 * ((down & 127) >> 3) + 512 * ((across & 127) >> 4)
        table[d : d + 1, :] = listed(arrives, code)
        table[8 + d : 9 + d, :] = jnp.sum(jnp.where(arrives, 1, 0), axis=0, keepdims=True)
        rows = slice(d * PLANE, (d + 1) * PLANE)
        row_hot[rows, :] = jnp.where(((down & 127) >> 3) == lane, 1.0, 0.0)
        col_hot[rows, :] = jnp.where(owned & (((across & 127) >> 4) == lane), 1.0, 0.0)
        if d:
            goes = (y + d) & 3
            out = column(here, 4 * (goes & 1) + z)
            leaves = (((out >> 3) & 1) == (goes >> 1)) & (out > 127) & (mine > 127)
            table[3 + d : 4 + d, :] = listed(leaves, slot)
    most = jnp.max(need).astype(jnp.int32)
    level = 0
    for cap in CAPS[:-1]:
        level = level + jnp.where(most > cap, jnp.int32(1), jnp.int32(0))
    table[12:13, :] = jnp.zeros((1, TILE), jnp.int32) + level


def places(segments, all_wide):
    vectors = pl.BlockSpec(memory_space=pltpu.VMEM)
    return pl.pallas_call(
        places_kernel,
        in_specs=[vectors] * 2,
        out_specs=[vectors] * 3,
        out_shape=[
            jax.ShapeDtypeStruct((16, TILE), jnp.int32),
            jax.ShapeDtypeStruct((RING * PLANE, TILE), F32),
            jax.ShapeDtypeStruct((RING * PLANE, TILE), F32),
        ],
        scratch_shapes=[
            pltpu.VMEM((RING, PLANE, CLASSES), jnp.int32),
            pltpu.VMEM((RING, PLANE, TILE), jnp.int32),
        ],
        name="places",
    )(segments, all_wide)


def body(coupling, modes, flexibility, widths, segments):
    tiles, diag, all_wide = make_block(coupling, modes, flexibility, widths, segments)
    table, row_hot, col_hot = places(segments, all_wide)
    ring, own, diags = lax.switch(
        table[12, 0], [functools.partial(exchange, cap) for cap in CAPS], table, tiles, diag
    )
    out = assemble(table, ring, own, diags, row_hot, col_hot)
    return out.reshape(ROW_TILES * TILE, COL_TILES * TILE)


def solution(mesh):
    both = ("row", "col")
    return jax.shard_map(
        body,
        mesh=mesh,
        in_specs=(P(both, None, None), P(both, None, None), P(both, None), P(both), P()),
        out_specs=P("row", "col"),
        check_vma=False,
    )
```

```python
import functools

import jax
import jax.numpy as jnp
from jax import lax
from jax.experimental import pallas as pl
from jax.experimental.pallas import tpu as pltpu
from jax.sharding import PartitionSpec as P

TILE = 128
PARTS = (16,) * 8
AHEAD = 2
CLASSES = 8
PLANE = 32
RING = 4
ROW_TILES = 12
COL_TILES = 6
DEPTH = 1024
STEPS = 4
SPAN = 64
CAPS = (17, 18, 19, 20, 21, 23, PLANE)
F32 = jnp.float32
BF16 = jnp.bfloat16
MESH = pl.DeviceIdType.MESH
HIGH = lax.Precision.HIGHEST


def over_rows(left, right):
    return lax.dot_general(left, right, (((0,), (0,)), ((), ())), preferred_element_type=F32)


def block_kernel(segments, width, coupling, modes, weights, out, diag, all_wide, *scratch):
    wide, raw, mode_rows, tiles, acc, proj, m_sem, p_sem, w_sem, r_sem, t_sem = scratch
    row, col = lax.axis_index("row"), lax.axis_index("col")
    y, z = col // 4, col % 4
    mine = row * 4 + z

    def plane_peer(step):
        there = lax.rem(mine + step, PLANE)
        return (there // 4, y * 4 + lax.rem(there, 4))

    def ring_peer(step):
        return (row, lax.rem(y + step, RING) * 4 + z)

    def load(k):
        rows = pl.ds(k * DEPTH, DEPTH)
        return pltpu.make_async_copy(coupling.at[0, rows], raw.at[k], m_sem.at[k])

    mode_copy = pltpu.make_async_copy(modes.at[0], mode_rows, p_sem)
    load(0).start()
    mode_copy.start()
    for k in range(1, STEPS):
        load(k).start()
    barrier = pltpu.get_barrier_semaphore()

    def greet(step, carry):
        pl.semaphore_signal(barrier, inc=1, device_id=plane_peer(step), device_id_type=MESH)
        return carry

    lax.fori_loop(1, PLANE, greet, 0)
    for step in range(1, RING):
        pl.semaphore_signal(barrier, inc=1, device_id=ring_peer(step), device_id_type=MESH)
    wide[...] = jnp.zeros((1, TILE), F32) + width[0].astype(F32)
    acc[...] = jnp.zeros_like(acc)
    proj[...] = jnp.zeros_like(proj)
    here = pltpu.make_async_copy(wide, all_wide.at[y, mine], w_sem.at[2])

    def pass_on(step):
        return pltpu.make_async_remote_copy(
            src_ref=all_wide.at[y],
            dst_ref=all_wide.at[y],
            send_sem=r_sem.at[0, step - 1],
            recv_sem=r_sem.at[1, step - 1],
            device_id=ring_peer(step),
            device_id_type=MESH,
        )

    mode_copy.wait()

    def multiply(k, carry):
        load(k).wait()

        @pl.when(k == 1)
        def _():
            pl.semaphore_wait(barrier, PLANE - 1 + RING - 1)

            def tell(step, carry):
                pltpu.make_async_remote_copy(
                    src_ref=wide,
                    dst_ref=all_wide.at[y, mine],
                    send_sem=w_sem.at[0],
                    recv_sem=w_sem.at[1],
                    device_id=plane_peer(step),
                    device_id_type=MESH,
                ).start()
                return carry

            lax.fori_loop(1, PLANE, tell, 0)
            here.start()

        @pl.when(k == STEPS - 1)
        def _():
            others = all_wide.at[y, pl.ds(0, PLANE - 1)]
            pltpu.make_async_copy(others, others, w_sem.at[1]).wait()
            pltpu.make_async_copy(others, others, w_sem.at[0]).wait()
            here.wait()
            for step in range(1, RING):
                pass_on(step).start()

        cols = pl.ds(pl.multiple_of(k * DEPTH, DEPTH), DEPTH)
        proj[...] += jnp.dot(mode_rows[:, cols], raw[k], preferred_element_type=F32)
        for m in range(0, CLASSES, 2):
            part = over_rows(raw[k, :, m * TILE : (m + 2) * TILE], raw[k, :, m * TILE :])
            for i in range(2):
                for n in range(m, CLASSES):
                    inside = part[i * TILE : (i + 1) * TILE, (n - m) * TILE : (n - m + 1) * TILE]
                    acc[m + i, n] += inside
        return carry

    lax.fori_loop(0, STEPS, multiply, 0)
    p = proj[...]
    count = p.shape[0]
    square = lax.broadcasted_iota(jnp.int32, (count, count), 0) == lax.broadcasted_iota(
        jnp.int32, (count, count), 1
    )
    w = p * jnp.sum(jnp.where(square, weights[...], 0.0), axis=1, keepdims=True)
    p_hi, w_hi = p.astype(BF16), w.astype(BF16)
    p_lo = (p - p_hi.astype(F32)).astype(BF16)
    w_lo = (w - w_hi.astype(F32)).astype(BF16)
    left = jnp.concatenate([w_hi, w_hi, w_lo], 0)
    right = jnp.concatenate([p_hi, p_lo, p_hi], 0)
    for m in range(0, CLASSES, 2):
        part = over_rows(left[:, m * TILE : (m + 2) * TILE], right[:, m * TILE :])
        for i in range(2):
            for n in range(m, CLASSES):
                inside = part[i * TILE : (i + 1) * TILE, (n - m) * TILE : (n - m + 1) * TILE]
                tile = acc[m + i, n] - inside
                acc[m + i, n] = tile
                if n > m + 1:
                    acc[n, m + i] = tile.T
    perm = []
    for k in range(CLASSES):
        place = jnp.int32(0)
        for j in range(1, CLASSES):
            fits = (segments[0, j] & 7) == k
            place = jnp.where(fits, jnp.int32(j), place)
        perm.append(place)
    down = lax.broadcasted_iota(jnp.int32, (TILE, TILE), 0)
    across = lax.broadcasted_iota(jnp.int32, (TILE, TILE), 1)
    copies = []
    for k in range(CLASSES):
        above = down < width[0] - perm[k] * TILE
        for m in range(CLASSES):
            inside = above & (across < width[0] - perm[m] * TILE)
            tile = jnp.where(inside, acc[perm[k], perm[m]], 0.0)
            tiles[k, m % 4, m // 4] = tile
            if k == m:
                diag[k : k + 1, :] = jnp.sum(
                    jnp.where(down == across, tile, 0.0), axis=0, keepdims=True
                )
        copy = pltpu.make_async_copy(tiles.at[k], out.at[k], t_sem.at[k])
        copy.start()
        copies.append(copy)
    for step in range(1, RING):
        pass_on(step).wait()
    for copy in copies:
        copy.wait()


def make_block(coupling, modes, flexibility, width, segments):
    count = modes.shape[1]
    dma = pltpu.SemaphoreType.DMA
    scalars = pl.BlockSpec(memory_space=pltpu.SMEM)
    far, vectors = pl.BlockSpec(memory_space=pltpu.HBM), pl.BlockSpec(memory_space=pltpu.VMEM)
    return pl.pallas_call(
        block_kernel,
        in_specs=[scalars, scalars, far, far, vectors],
        out_specs=[pl.BlockSpec(memory_space=pl.ANY), vectors, vectors],
        out_shape=[
            jax.ShapeDtypeStruct((8, 4, 2, TILE, TILE), F32),
            jax.ShapeDtypeStruct((CLASSES, TILE), F32),
            jax.ShapeDtypeStruct((RING, PLANE, 1, TILE), F32),
        ],
        scratch_shapes=[
            pltpu.VMEM((1, TILE), F32),
            pltpu.VMEM((STEPS, DEPTH, 1024), BF16),
            pltpu.VMEM((count, 4096), BF16),
            pltpu.VMEM((8, 4, 2, TILE, TILE), F32),
            pltpu.VMEM((CLASSES, CLASSES, TILE, TILE), F32),
            pltpu.VMEM((count, 1024), F32),
            dma((STEPS,)),
            dma,
            dma((3,)),
            dma((2, RING - 1)),
            dma((CLASSES,)),
        ],
        compiler_params=pltpu.CompilerParams(
            collective_id=1, has_side_effects=True, vmem_limit_bytes=60 << 20
        ),
        name="block",
    )(segments, width, coupling, modes, flexibility)


def exchange_kernel(cap, table, tiles, diag, ring_out, own_out, diag_out, *scratch):
    chunks = len(PARTS)
    held, send, scratch = scratch[:chunks], scratch[chunks : 2 * chunks], scratch[2 * chunks :]
    spans = [pl.ds(sum(PARTS[:q]), PARTS[q]) for q in range(chunks)]
    diag_held, diag_send, a_send, a_recv, b_send, b_recv, o_sem, d_sem = scratch
    row, col = lax.axis_index("row"), lax.axis_index("col")
    y, z = col // 4, col % 4
    mine = row * 4 + z

    def plane_peer(step):
        there = lax.rem(mine + step, PLANE)
        return there, (there // 4, y * 4 + lax.rem(there, 4))

    def ring_peer(step):
        return (row, lax.rem(y + step, RING) * 4 + z)

    barrier = pltpu.get_barrier_semaphore()

    def greet(step, carry):
        pl.semaphore_signal(barrier, inc=1, device_id=plane_peer(step)[1], device_id_type=MESH)
        return carry

    lax.fori_loop(1, PLANE, greet, 0)
    for step in range(1, RING):
        pl.semaphore_signal(barrier, inc=1, device_id=ring_peer(step), device_id_type=MESH)
    pl.semaphore_wait(barrier, PLANE - 1 + RING - 1)

    own_copies, kept = [None] * chunks, []

    def local(src, dst, sem):
        copy = pltpu.make_async_copy(src, dst, sem)
        copy.start()
        return copy

    def send_diag(step, carry):
        pltpu.make_async_remote_copy(
            src_ref=diag,
            dst_ref=diag_held.at[mine],
            send_sem=d_sem.at[0],
            recv_sem=d_sem.at[1],
            device_id=plane_peer(step)[1],
            device_id_type=MESH,
        ).start()
        return carry

    def start_plane(q):
        def send_tiles(step, carry):
            there, peer = plane_peer(step)
            pltpu.make_async_remote_copy(
                src_ref=tiles.at[there // 4, lax.rem(there, 4), :, spans[q]],
                dst_ref=held[q].at[mine],
                send_sem=a_send.at[q],
                recv_sem=a_recv.at[q],
                device_id=peer,
                device_id_type=MESH,
            ).start()
            return carry

        lax.fori_loop(1, PLANE, send_tiles, 0)
        own_copies[q] = local(tiles.at[row, z, :, spans[q]], held[q].at[mine], o_sem.at[0, q])

    def whole(ref, sem):
        part = ref.at[pl.ds(0, PLANE - 1)]
        pltpu.make_async_copy(part, part, sem).wait()

    pending = []
    for q in range(AHEAD):
        start_plane(q)
    for q in range(chunks):
        whole(held[q], a_recv.at[q])
        own_copies[q].wait()
        for step in range(1, RING):
            parity = lax.rem(y + step, 2)

            def arrange(j, carry, q=q, step=step, parity=parity):
                send[q][step - 1, j] = held[q][table[3 + step, j], parity]
                return carry

            lax.fori_loop(0, cap, arrange, 0)
            copy = pltpu.make_async_remote_copy(
                src_ref=send[q].at[step - 1],
                dst_ref=ring_out.at[step - 1, pl.ds(0, cap), spans[q]],
                send_sem=b_send.at[q, step - 1],
                recv_sem=b_recv.at[q, step - 1],
                device_id=ring_peer(step),
                device_id_type=MESH,
            )
            copy.start()
            pending.append(copy)
        kept.append(local(held[q].at[:, lax.rem(y, 2)], own_out.at[:, spans[q]], o_sem.at[1, q]))
        if q + AHEAD < chunks:
            start_plane(q + AHEAD)
        if q == 1:
            own_diag = local(diag, diag_held.at[mine], d_sem.at[2])
            lax.fori_loop(1, PLANE, send_diag, 0)
        if q == 4:
            whole(diag_held, d_sem.at[1])
            own_diag.wait()

            def pick(i, carry):
                for parity in range(2):
                    diag_send[parity, 0, pl.ds(i, 1), :] = diag_held[i, pl.ds(row, 1), :]
                    diag_send[parity, 1, pl.ds(i, 1), :] = diag_held[i, pl.ds(4 * parity + z, 1), :]
                return carry

            lax.fori_loop(0, PLANE, pick, 0)
            here = local(diag_send.at[lax.rem(y, 2)], diag_out.at[0], d_sem.at[3])
            for step in range(1, RING):
                copy = pltpu.make_async_remote_copy(
                    src_ref=diag_send.at[lax.rem(y + step, 2)],
                    dst_ref=diag_out.at[step],
                    send_sem=b_send.at[chunks, step - 1],
                    recv_sem=b_recv.at[chunks, step - 1],
                    device_id=ring_peer(step),
                    device_id_type=MESH,
                )
                copy.start()
                pending.append(copy)
    for copy in pending:
        copy.wait()
    for copy in kept:
        copy.wait()
    here.wait()
    whole(diag_held, d_sem.at[0])
    for q in range(chunks):
        whole(held[q], a_send.at[q])


def exchange(cap, table, tiles, diag):
    dma = pltpu.SemaphoreType.DMA
    anywhere = pl.BlockSpec(memory_space=pl.ANY)
    return pl.pallas_call(
        functools.partial(exchange_kernel, cap),
        in_specs=[pl.BlockSpec(memory_space=pltpu.SMEM), anywhere, anywhere],
        out_specs=[anywhere] * 3,
        out_shape=[
            jax.ShapeDtypeStruct((RING - 1, PLANE, TILE, TILE), F32),
            jax.ShapeDtypeStruct((PLANE, TILE, TILE), F32),
            jax.ShapeDtypeStruct((RING, 2, PLANE, TILE), F32),
        ],
        scratch_shapes=[pltpu.VMEM((PLANE, 2, part, TILE), F32) for part in PARTS]
        + [pltpu.VMEM((RING - 1, cap, part, TILE), F32) for part in PARTS]
        + [
            pltpu.VMEM((PLANE, CLASSES, TILE), F32),
            pltpu.VMEM((2, 2, PLANE, TILE), F32),
            dma((len(PARTS),)),
            dma((len(PARTS),)),
            dma((len(PARTS) + 1, RING - 1)),
            dma((len(PARTS) + 1, RING - 1)),
            dma((2, len(PARTS))),
            dma((4,)),
        ],
        compiler_params=pltpu.CompilerParams(
            collective_id=cap + 1, has_side_effects=True, vmem_limit_bytes=40 << 20
        ),
        name="exchange",
    )(table, tiles, diag)


def exactly(left, right):
    return lax.dot_general(
        left, right, (((0,), (0,)), ((), ())), precision=HIGH, preferred_element_type=F32
    )


def assemble_kernel(table, ring, own, diag, row_hot, col_hot, out, row_scale, col_scale, acc, sem):
    rows = exactly(diag[:, 0].reshape(RING * PLANE, TILE), row_hot[...])
    cols = exactly(col_hot[...], diag[:, 1].reshape(RING * PLANE, TILE))[:8]
    row_scale[...] = 1.0 / jnp.sqrt(1.0 + jnp.abs(rows))
    col_scale[...] = 1.0 / jnp.sqrt(1.0 + jnp.abs(cols))
    copies = []
    for first in range(0, TILE, SPAN):
        span = slice(first, first + SPAN)
        acc[:, span] = jnp.zeros((ROW_TILES, SPAN, COL_TILES * TILE), F32)
        for d in range(RING):

            def add(j, carry, d=d, span=span):
                code = table[d, j]
                tile = own[code & 31, span] if d == 0 else ring[d - 1, j, span]
                across = pl.ds(pl.multiple_of((code >> 9) * TILE, TILE), TILE)
                acc[(code >> 5) & 15, span, across] += tile
                return carry

            lax.fori_loop(0, table[8 + d, 0], add, 0)
        for g in range(ROW_TILES):
            down = jnp.broadcast_to(row_scale[span, g : g + 1], (SPAN, TILE))
            for h in range(COL_TILES):
                acc[g, span, h * TILE : (h + 1) * TILE] *= down * col_scale[h : h + 1, :]
        copy = pltpu.make_async_copy(acc.at[:, span], out.at[:, span], sem.at[first // SPAN])
        copy.start()
        copies.append(copy)
    for copy in copies:
        copy.wait()


def assemble(table, ring, own, diag, row_hot, col_hot):
    scalars, vectors = pl.BlockSpec(memory_space=pltpu.SMEM), pl.BlockSpec(memory_space=pltpu.VMEM)
    shape = (ROW_TILES, TILE, COL_TILES * TILE)
    return pl.pallas_call(
        assemble_kernel,
        in_specs=[scalars] + [vectors] * 5,
        out_specs=pl.BlockSpec(memory_space=pl.ANY),
        out_shape=jax.ShapeDtypeStruct(shape, F32),
        scratch_shapes=[
            pltpu.VMEM((TILE, TILE), F32),
            pltpu.VMEM((8, TILE), F32),
            pltpu.VMEM(shape, F32),
            pltpu.SemaphoreType.DMA((TILE // SPAN,)),
        ],
        compiler_params=pltpu.CompilerParams(vmem_limit_bytes=24 << 20),
        name="assemble",
    )(table, ring, own, diag, row_hot, col_hot)


def places_kernel(segments, all_wide, table, row_hot, col_hot, choice, plane, tags):
    row, col = lax.axis_index("row"), lax.axis_index("col")
    y, z = col // 4, col % 4
    lane = lax.broadcasted_iota(jnp.int32, (PLANE, TILE), 1)
    slot = lax.broadcasted_iota(jnp.int32, (PLANE, TILE), 0)
    lane8 = lax.broadcasted_iota(jnp.int32, (PLANE, CLASSES), 1)
    need = jnp.zeros((CLASSES, TILE), F32)
    half = lax.broadcasted_iota(jnp.int32, (CLASSES, TILE), 0) >> 2
    for p in range(RING):
        for k in range(CLASSES):
            first = 16 * k + 4 * p
            plane[p, 4 * k : 4 * k + 4, :] = segments[first : first + 4, :]
        numbers = plane[p]
        width = all_wide[p, :, 0, :].astype(jnp.int32)
        tag = jnp.zeros((PLANE, TILE), jnp.int32)
        for k in range(CLASSES):
            found = jnp.where((numbers & 7) == k, numbers + 128 * lane8, 0)
            found = jnp.broadcast_to(jnp.sum(found, axis=1, keepdims=True), (PLANE, TILE))
            used = jnp.where((found >> 7) * TILE < width, 128, 0)
            tag = jnp.where(lane == k, (found & 127) + used, tag)
        tags[p] = tag
        filled = (tag >> 7).astype(F32)
        high = ((tag >> 3) & 1).astype(F32)
        for h, part in ((0, filled * (1.0 - high)), (1, filled * high)):
            held = over_rows(part, filled)[:CLASSES]
            need = jnp.maximum(need, jnp.where(2 * h + half == p, 0.0, held))

    def column(values, index):
        picked = jnp.sum(jnp.where(lane == index, values, 0), axis=1, keepdims=True)
        return jnp.broadcast_to(picked, (PLANE, TILE))

    earlier = lax.broadcasted_iota(jnp.int32, (PLANE, PLANE), 0) > lax.broadcasted_iota(
        jnp.int32, (PLANE, PLANE), 1
    )
    earlier = jnp.where(earlier, 1.0, 0.0).astype(F32)

    def listed(flag, values):
        rank = jnp.dot(earlier, jnp.where(flag, 1.0, 0.0), preferred_element_type=F32)
        lands = flag & (rank.astype(jnp.int32) == lane)
        return jnp.sum(jnp.where(lands, values, 0), axis=0, keepdims=True)

    table[...] = jnp.zeros((16, TILE), jnp.int32)
    here = tags[y]
    mine = column(here, row)
    for d in range(RING):
        tag = tags[(y - d) & 3]
        down, across = column(tag, row), column(tag, col & 7)
        owned = ((across >> 3) & 1) == (col >> 3)
        arrives = owned & (down > 127) & (across > 127)
        code = slot + 32 * ((down & 127) >> 3) + 512 * ((across & 127) >> 4)
        table[d : d + 1, :] = listed(arrives, code)
        table[8 + d : 9 + d, :] = jnp.sum(jnp.where(arrives, 1, 0), axis=0, keepdims=True)
        rows = slice(d * PLANE, (d + 1) * PLANE)
        row_hot[rows, :] = jnp.where(((down & 127) >> 3) == lane, 1.0, 0.0)
        col_hot[rows, :] = jnp.where(owned & (((across & 127) >> 4) == lane), 1.0, 0.0)
        if d:
            goes = (y + d) & 3
            out = column(here, 4 * (goes & 1) + z)
            leaves = (((out >> 3) & 1) == (goes >> 1)) & (out > 127) & (mine > 127)
            table[3 + d : 4 + d, :] = listed(leaves, slot)
    most = jnp.max(need).astype(jnp.int32)
    level = 0
    for cap in CAPS[:-1]:
        level = level + jnp.where(most > cap, jnp.int32(1), jnp.int32(0))
    choice[0] = level


def places(segments, all_wide):
    vectors = pl.BlockSpec(memory_space=pltpu.VMEM)
    return pl.pallas_call(
        places_kernel,
        in_specs=[vectors] * 2,
        out_specs=[vectors] * 3 + [pl.BlockSpec(memory_space=pltpu.SMEM)],
        out_shape=[
            jax.ShapeDtypeStruct((16, TILE), jnp.int32),
            jax.ShapeDtypeStruct((RING * PLANE, TILE), F32),
            jax.ShapeDtypeStruct((RING * PLANE, TILE), F32),
            jax.ShapeDtypeStruct((1,), jnp.int32),
        ],
        scratch_shapes=[
            pltpu.VMEM((RING, PLANE, CLASSES), jnp.int32),
            pltpu.VMEM((RING, PLANE, TILE), jnp.int32),
        ],
        name="places",
    )(segments, all_wide)


def body(coupling, modes, flexibility, widths, segments):
    device = lax.axis_index("row") * 16 + lax.axis_index("col")
    own_segments = lax.dynamic_slice_in_dim(segments, device, 1, 0)
    tiles, diag, all_wide = make_block(coupling, modes, flexibility, widths, own_segments)
    table, row_hot, col_hot, choice = places(segments, all_wide)
    ring, own, diags = lax.switch(
        choice[0], [functools.partial(exchange, cap) for cap in CAPS], table, tiles, diag
    )
    out = assemble(table, ring, own, diags, row_hot, col_hot)
    return out.reshape(ROW_TILES * TILE, COL_TILES * TILE)


def solution(mesh):
    both = ("row", "col")
    return jax.shard_map(
        body,
        mesh=mesh,
        in_specs=(P(both, None, None), P(both, None, None), P(both, None), P(both), P()),
        out_specs=P("row", "col"),
        check_vma=False,
    )
```

```python
import functools

import jax
import jax.numpy as jnp
from jax import lax
from jax.experimental import pallas as pl
from jax.experimental.pallas import tpu as pltpu
from jax.sharding import PartitionSpec as P

TILE = 128
PARTS = (16,) * 8
AHEAD = 2
CLASSES = 8
PLANE = 32
RING = 4
ROW_TILES = 12
COL_TILES = 6
DEPTH = 1024
STEPS = 4
SPAN = 64
CAPS = (17, 18, 19, 20, 21, 22, 25, PLANE)
F32 = jnp.float32
BF16 = jnp.bfloat16
MESH = pl.DeviceIdType.MESH
HIGH = lax.Precision.HIGHEST


def over_rows(left, right):
    return lax.dot_general(left, right, (((0,), (0,)), ((), ())), preferred_element_type=F32)


def block_kernel(segments, width, coupling, modes, weights, out, diag, all_wide, *scratch):
    wide, raw, mode_rows, tiles, acc, proj, m_sem, p_sem, w_sem, r_sem, t_sem = scratch
    row, col = lax.axis_index("row"), lax.axis_index("col")
    y, z = col // 4, col % 4
    mine = row * 4 + z

    def plane_peer(step):
        there = lax.rem(mine + step, PLANE)
        return (there // 4, y * 4 + lax.rem(there, 4))

    def ring_peer(step):
        return (row, lax.rem(y + step, RING) * 4 + z)

    def load(k):
        rows = pl.ds(k * DEPTH, DEPTH)
        return pltpu.make_async_copy(coupling.at[0, rows], raw.at[k], m_sem.at[k])

    mode_copy = pltpu.make_async_copy(modes.at[0], mode_rows, p_sem)
    load(0).start()
    mode_copy.start()
    for k in range(1, STEPS):
        load(k).start()
    barrier = pltpu.get_barrier_semaphore()

    def greet(step, carry):
        pl.semaphore_signal(barrier, inc=1, device_id=plane_peer(step), device_id_type=MESH)
        return carry

    lax.fori_loop(1, PLANE, greet, 0)
    for step in range(1, RING):
        pl.semaphore_signal(barrier, inc=1, device_id=ring_peer(step), device_id_type=MESH)
    wide[...] = jnp.zeros((1, TILE), F32) + width[0].astype(F32)
    acc[...] = jnp.zeros_like(acc)
    proj[...] = jnp.zeros_like(proj)
    here = pltpu.make_async_copy(wide, all_wide.at[y, mine], w_sem.at[2])

    def pass_on(step):
        return pltpu.make_async_remote_copy(
            src_ref=all_wide.at[y],
            dst_ref=all_wide.at[y],
            send_sem=r_sem.at[0, step - 1],
            recv_sem=r_sem.at[1, step - 1],
            device_id=ring_peer(step),
            device_id_type=MESH,
        )

    mode_copy.wait()

    def multiply(k, carry):
        load(k).wait()

        @pl.when(k == 1)
        def _():
            pl.semaphore_wait(barrier, PLANE - 1 + RING - 1)

            def tell(step, carry):
                pltpu.make_async_remote_copy(
                    src_ref=wide,
                    dst_ref=all_wide.at[y, mine],
                    send_sem=w_sem.at[0],
                    recv_sem=w_sem.at[1],
                    device_id=plane_peer(step),
                    device_id_type=MESH,
                ).start()
                return carry

            lax.fori_loop(1, PLANE, tell, 0)
            here.start()

        @pl.when(k == STEPS - 1)
        def _():
            others = all_wide.at[y, pl.ds(0, PLANE - 1)]
            pltpu.make_async_copy(others, others, w_sem.at[1]).wait()
            pltpu.make_async_copy(others, others, w_sem.at[0]).wait()
            here.wait()
            for step in range(1, RING):
                pass_on(step).start()

        cols = pl.ds(pl.multiple_of(k * DEPTH, DEPTH), DEPTH)
        proj[...] += jnp.dot(mode_rows[:, cols], raw[k], preferred_element_type=F32)
        for m in range(0, CLASSES, 2):
            part = over_rows(raw[k, :, m * TILE : (m + 2) * TILE], raw[k, :, m * TILE :])
            for i in range(2):
                for n in range(m, CLASSES):
                    inside = part[i * TILE : (i + 1) * TILE, (n - m) * TILE : (n - m + 1) * TILE]
                    acc[m + i, n] += inside
        return carry

    lax.fori_loop(0, STEPS, multiply, 0)
    p = proj[...]
    count = p.shape[0]
    square = lax.broadcasted_iota(jnp.int32, (count, count), 0) == lax.broadcasted_iota(
        jnp.int32, (count, count), 1
    )
    w = p * jnp.sum(jnp.where(square, weights[...], 0.0), axis=1, keepdims=True)
    p_hi, w_hi = p.astype(BF16), w.astype(BF16)
    p_lo = (p - p_hi.astype(F32)).astype(BF16)
    w_lo = (w - w_hi.astype(F32)).astype(BF16)
    left = jnp.concatenate([w_hi, w_hi, w_lo], 0)
    right = jnp.concatenate([p_hi, p_lo, p_hi], 0)
    for m in range(0, CLASSES, 2):
        part = over_rows(left[:, m * TILE : (m + 2) * TILE], right[:, m * TILE :])
        for i in range(2):
            for n in range(m, CLASSES):
                inside = part[i * TILE : (i + 1) * TILE, (n - m) * TILE : (n - m + 1) * TILE]
                tile = acc[m + i, n] - inside
                acc[m + i, n] = tile
                if n > m + 1:
                    acc[n, m + i] = tile.T
    perm = []
    for k in range(CLASSES):
        place = jnp.int32(0)
        for j in range(1, CLASSES):
            fits = (segments[0, j] & 7) == k
            place = jnp.where(fits, jnp.int32(j), place)
        perm.append(place)
    down = lax.broadcasted_iota(jnp.int32, (TILE, TILE), 0)
    across = lax.broadcasted_iota(jnp.int32, (TILE, TILE), 1)
    copies = []
    for k in range(CLASSES):
        above = down < width[0] - perm[k] * TILE
        for m in range(CLASSES):
            inside = above & (across < width[0] - perm[m] * TILE)
            tile = jnp.where(inside, acc[perm[k], perm[m]], 0.0)
            tiles[k, m % 4, m // 4] = tile
            if k == m:
                diag[k : k + 1, :] = jnp.sum(
                    jnp.where(down == across, tile, 0.0), axis=0, keepdims=True
                )
        copy = pltpu.make_async_copy(tiles.at[k], out.at[k], t_sem.at[k])
        copy.start()
        copies.append(copy)
    for step in range(1, RING):
        pass_on(step).wait()
    for copy in copies:
        copy.wait()


def make_block(coupling, modes, flexibility, width, segments):
    count = modes.shape[1]
    dma = pltpu.SemaphoreType.DMA
    scalars = pl.BlockSpec(memory_space=pltpu.SMEM)
    far, vectors = pl.BlockSpec(memory_space=pltpu.HBM), pl.BlockSpec(memory_space=pltpu.VMEM)
    return pl.pallas_call(
        block_kernel,
        in_specs=[scalars, scalars, far, far, vectors],
        out_specs=[pl.BlockSpec(memory_space=pl.ANY), vectors, vectors],
        out_shape=[
            jax.ShapeDtypeStruct((8, 4, 2, TILE, TILE), F32),
            jax.ShapeDtypeStruct((CLASSES, TILE), F32),
            jax.ShapeDtypeStruct((RING, PLANE, 1, TILE), F32),
        ],
        scratch_shapes=[
            pltpu.VMEM((1, TILE), F32),
            pltpu.VMEM((STEPS, DEPTH, 1024), BF16),
            pltpu.VMEM((count, 4096), BF16),
            pltpu.VMEM((8, 4, 2, TILE, TILE), F32),
            pltpu.VMEM((CLASSES, CLASSES, TILE, TILE), F32),
            pltpu.VMEM((count, 1024), F32),
            dma((STEPS,)),
            dma,
            dma((3,)),
            dma((2, RING - 1)),
            dma((CLASSES,)),
        ],
        compiler_params=pltpu.CompilerParams(
            collective_id=1, has_side_effects=True, vmem_limit_bytes=60 << 20
        ),
        name="block",
    )(segments, width, coupling, modes, flexibility)


def exchange_kernel(cap, table, tiles, diag, ring_out, own_out, diag_out, *scratch):
    chunks = len(PARTS)
    held, send, scratch = scratch[:chunks], scratch[chunks : 2 * chunks], scratch[2 * chunks :]
    spans = [pl.ds(sum(PARTS[:q]), PARTS[q]) for q in range(chunks)]
    diag_held, diag_send, a_send, a_recv, b_send, b_recv, o_sem, d_sem = scratch
    row, col = lax.axis_index("row"), lax.axis_index("col")
    y, z = col // 4, col % 4
    mine = row * 4 + z

    def plane_peer(step):
        there = lax.rem(mine + step, PLANE)
        return there, (there // 4, y * 4 + lax.rem(there, 4))

    def ring_peer(step):
        return (row, lax.rem(y + step, RING) * 4 + z)

    barrier = pltpu.get_barrier_semaphore()

    def greet(step, carry):
        pl.semaphore_signal(barrier, inc=1, device_id=plane_peer(step)[1], device_id_type=MESH)
        return carry

    lax.fori_loop(1, PLANE, greet, 0)
    for step in range(1, RING):
        pl.semaphore_signal(barrier, inc=1, device_id=ring_peer(step), device_id_type=MESH)
    pl.semaphore_wait(barrier, PLANE - 1 + RING - 1)

    own_copies, kept = [None] * chunks, []

    def local(src, dst, sem):
        copy = pltpu.make_async_copy(src, dst, sem)
        copy.start()
        return copy

    def send_diag(step, carry):
        pltpu.make_async_remote_copy(
            src_ref=diag,
            dst_ref=diag_held.at[mine],
            send_sem=d_sem.at[0],
            recv_sem=d_sem.at[1],
            device_id=plane_peer(step)[1],
            device_id_type=MESH,
        ).start()
        return carry

    def start_plane(q):
        def send_tiles(step, carry):
            there, peer = plane_peer(step)
            pltpu.make_async_remote_copy(
                src_ref=tiles.at[there // 4, lax.rem(there, 4), :, spans[q]],
                dst_ref=held[q].at[mine],
                send_sem=a_send.at[q],
                recv_sem=a_recv.at[q],
                device_id=peer,
                device_id_type=MESH,
            ).start()
            return carry

        lax.fori_loop(1, PLANE, send_tiles, 0)
        own_copies[q] = local(tiles.at[row, z, :, spans[q]], held[q].at[mine], o_sem.at[0, q])

    def whole(ref, sem):
        part = ref.at[pl.ds(0, PLANE - 1)]
        pltpu.make_async_copy(part, part, sem).wait()

    pending = []
    for q in range(AHEAD):
        start_plane(q)
    for q in range(chunks):
        whole(held[q], a_recv.at[q])
        own_copies[q].wait()
        for step in range(1, RING):
            parity = lax.rem(y + step, 2)

            def arrange(j, carry, q=q, step=step, parity=parity):
                send[q][step - 1, j] = held[q][table[3 + step, j], parity]
                return carry

            lax.fori_loop(0, cap, arrange, 0)
            copy = pltpu.make_async_remote_copy(
                src_ref=send[q].at[step - 1],
                dst_ref=ring_out.at[step - 1, pl.ds(0, cap), spans[q]],
                send_sem=b_send.at[q, step - 1],
                recv_sem=b_recv.at[q, step - 1],
                device_id=ring_peer(step),
                device_id_type=MESH,
            )
            copy.start()
            pending.append(copy)
        kept.append(local(held[q].at[:, lax.rem(y, 2)], own_out.at[:, spans[q]], o_sem.at[1, q]))
        if q + AHEAD < chunks:
            start_plane(q + AHEAD)
        if q == 1:
            own_diag = local(diag, diag_held.at[mine], d_sem.at[2])
            lax.fori_loop(1, PLANE, send_diag, 0)
        if q == 4:
            whole(diag_held, d_sem.at[1])
            own_diag.wait()

            def pick(i, carry):
                for parity in range(2):
                    diag_send[parity, 0, pl.ds(i, 1), :] = diag_held[i, pl.ds(row, 1), :]
                    diag_send[parity, 1, pl.ds(i, 1), :] = diag_held[i, pl.ds(4 * parity + z, 1), :]
                return carry

            lax.fori_loop(0, PLANE, pick, 0)
            here = local(diag_send.at[lax.rem(y, 2)], diag_out.at[0], d_sem.at[3])
            for step in range(1, RING):
                copy = pltpu.make_async_remote_copy(
                    src_ref=diag_send.at[lax.rem(y + step, 2)],
                    dst_ref=diag_out.at[step],
                    send_sem=b_send.at[chunks, step - 1],
                    recv_sem=b_recv.at[chunks, step - 1],
                    device_id=ring_peer(step),
                    device_id_type=MESH,
                )
                copy.start()
                pending.append(copy)
    for copy in pending:
        copy.wait()
    for copy in kept:
        copy.wait()
    here.wait()
    whole(diag_held, d_sem.at[0])
    for q in range(chunks):
        whole(held[q], a_send.at[q])


def exchange(cap, table, tiles, diag):
    dma = pltpu.SemaphoreType.DMA
    anywhere = pl.BlockSpec(memory_space=pl.ANY)
    return pl.pallas_call(
        functools.partial(exchange_kernel, cap),
        in_specs=[pl.BlockSpec(memory_space=pltpu.SMEM), anywhere, anywhere],
        out_specs=[anywhere] * 3,
        out_shape=[
            jax.ShapeDtypeStruct((RING - 1, PLANE, TILE, TILE), F32),
            jax.ShapeDtypeStruct((PLANE, TILE, TILE), F32),
            jax.ShapeDtypeStruct((RING, 2, PLANE, TILE), F32),
        ],
        scratch_shapes=[pltpu.VMEM((PLANE, 2, part, TILE), F32) for part in PARTS]
        + [pltpu.VMEM((RING - 1, cap, part, TILE), F32) for part in PARTS]
        + [
            pltpu.VMEM((PLANE, CLASSES, TILE), F32),
            pltpu.VMEM((2, 2, PLANE, TILE), F32),
            dma((len(PARTS),)),
            dma((len(PARTS),)),
            dma((len(PARTS) + 1, RING - 1)),
            dma((len(PARTS) + 1, RING - 1)),
            dma((2, len(PARTS))),
            dma((4,)),
        ],
        compiler_params=pltpu.CompilerParams(
            collective_id=cap + 1, has_side_effects=True, vmem_limit_bytes=40 << 20
        ),
        name="exchange",
    )(table, tiles, diag)


def exactly(left, right):
    return lax.dot_general(
        left, right, (((0,), (0,)), ((), ())), precision=HIGH, preferred_element_type=F32
    )


def assemble_kernel(table, ring, own, diag, row_hot, col_hot, out, row_scale, col_scale, acc, sem):
    rows = exactly(diag[:, 0].reshape(RING * PLANE, TILE), row_hot[...])
    cols = exactly(col_hot[...], diag[:, 1].reshape(RING * PLANE, TILE))[:8]
    row_scale[...] = 1.0 / jnp.sqrt(1.0 + jnp.abs(rows))
    col_scale[...] = 1.0 / jnp.sqrt(1.0 + jnp.abs(cols))
    copies = []
    for first in range(0, TILE, SPAN):
        span = slice(first, first + SPAN)
        acc[:, span] = jnp.zeros((ROW_TILES, SPAN, COL_TILES * TILE), F32)
        for d in range(RING):

            def add(j, carry, d=d, span=span):
                code = table[d, j]
                tile = own[code & 31, span] if d == 0 else ring[d - 1, j, span]
                across = pl.ds(pl.multiple_of((code >> 9) * TILE, TILE), TILE)
                acc[(code >> 5) & 15, span, across] += tile
                return carry

            lax.fori_loop(0, table[8 + d, 0], add, 0)
        for g in range(ROW_TILES):
            down = jnp.broadcast_to(row_scale[span, g : g + 1], (SPAN, TILE))
            for h in range(COL_TILES):
                acc[g, span, h * TILE : (h + 1) * TILE] *= down * col_scale[h : h + 1, :]
        copy = pltpu.make_async_copy(acc.at[:, span], out.at[:, span], sem.at[first // SPAN])
        copy.start()
        copies.append(copy)
    for copy in copies:
        copy.wait()


def assemble(table, ring, own, diag, row_hot, col_hot):
    scalars, vectors = pl.BlockSpec(memory_space=pltpu.SMEM), pl.BlockSpec(memory_space=pltpu.VMEM)
    shape = (ROW_TILES, TILE, COL_TILES * TILE)
    return pl.pallas_call(
        assemble_kernel,
        in_specs=[scalars] + [vectors] * 5,
        out_specs=pl.BlockSpec(memory_space=pl.ANY),
        out_shape=jax.ShapeDtypeStruct(shape, F32),
        scratch_shapes=[
            pltpu.VMEM((TILE, TILE), F32),
            pltpu.VMEM((8, TILE), F32),
            pltpu.VMEM(shape, F32),
            pltpu.SemaphoreType.DMA((TILE // SPAN,)),
        ],
        compiler_params=pltpu.CompilerParams(vmem_limit_bytes=24 << 20),
        name="assemble",
    )(table, ring, own, diag, row_hot, col_hot)


def places_kernel(segments, all_wide, table, row_hot, col_hot, choice, plane, tags):
    row, col = lax.axis_index("row"), lax.axis_index("col")
    y, z = col // 4, col % 4
    lane = lax.broadcasted_iota(jnp.int32, (PLANE, TILE), 1)
    slot = lax.broadcasted_iota(jnp.int32, (PLANE, TILE), 0)
    lane8 = lax.broadcasted_iota(jnp.int32, (PLANE, CLASSES), 1)
    need = jnp.zeros((CLASSES, TILE), F32)
    half = lax.broadcasted_iota(jnp.int32, (CLASSES, TILE), 0) >> 2
    for p in range(RING):
        for k in range(CLASSES):
            first = 16 * k + 4 * p
            plane[p, 4 * k : 4 * k + 4, :] = segments[first : first + 4, :]
        numbers = plane[p]
        width = all_wide[p, :, 0, :].astype(jnp.int32)
        tag = jnp.zeros((PLANE, TILE), jnp.int32)
        for k in range(CLASSES):
            found = jnp.where((numbers & 7) == k, numbers + 128 * lane8, 0)
            found = jnp.broadcast_to(jnp.sum(found, axis=1, keepdims=True), (PLANE, TILE))
            used = jnp.where((found >> 7) * TILE < width, 128, 0)
            tag = jnp.where(lane == k, (found & 127) + used, tag)
        tags[p] = tag
        filled = (tag >> 7).astype(F32)
        high = ((tag >> 3) & 1).astype(F32)
        for h, part in ((0, filled * (1.0 - high)), (1, filled * high)):
            held = over_rows(part, filled)[:CLASSES]
            need = jnp.maximum(need, jnp.where(2 * h + half == p, 0.0, held))

    def column(values, index):
        picked = jnp.sum(jnp.where(lane == index, values, 0), axis=1, keepdims=True)
        return jnp.broadcast_to(picked, (PLANE, TILE))

    earlier = lax.broadcasted_iota(jnp.int32, (PLANE, PLANE), 0) > lax.broadcasted_iota(
        jnp.int32, (PLANE, PLANE), 1
    )
    earlier = jnp.where(earlier, 1.0, 0.0).astype(F32)

    def listed(flag, values):
        rank = jnp.dot(earlier, jnp.where(flag, 1.0, 0.0), preferred_element_type=F32)
        lands = flag & (rank.astype(jnp.int32) == lane)
        return jnp.sum(jnp.where(lands, values, 0), axis=0, keepdims=True)

    table[...] = jnp.zeros((16, TILE), jnp.int32)
    here = tags[y]
    mine = column(here, row)
    for d in range(RING):
        tag = tags[(y - d) & 3]
        down, across = column(tag, row), column(tag, col & 7)
        owned = ((across >> 3) & 1) == (col >> 3)
        arrives = owned & (down > 127) & (across > 127)
        code = slot + 32 * ((down & 127) >> 3) + 512 * ((across & 127) >> 4)
        table[d : d + 1, :] = listed(arrives, code)
        table[8 + d : 9 + d, :] = jnp.sum(jnp.where(arrives, 1, 0), axis=0, keepdims=True)
        rows = slice(d * PLANE, (d + 1) * PLANE)
        row_hot[rows, :] = jnp.where(((down & 127) >> 3) == lane, 1.0, 0.0)
        col_hot[rows, :] = jnp.where(owned & (((across & 127) >> 4) == lane), 1.0, 0.0)
        if d:
            goes = (y + d) & 3
            out = column(here, 4 * (goes & 1) + z)
            leaves = (((out >> 3) & 1) == (goes >> 1)) & (out > 127) & (mine > 127)
            table[3 + d : 4 + d, :] = listed(leaves, slot)
    most = jnp.max(need).astype(jnp.int32)
    level = 0
    for cap in CAPS[:-1]:
        level = level + jnp.where(most > cap, jnp.int32(1), jnp.int32(0))
    choice[0] = level


def places(segments, all_wide):
    vectors = pl.BlockSpec(memory_space=pltpu.VMEM)
    return pl.pallas_call(
        places_kernel,
        in_specs=[vectors] * 2,
        out_specs=[vectors] * 3 + [pl.BlockSpec(memory_space=pltpu.SMEM)],
        out_shape=[
            jax.ShapeDtypeStruct((16, TILE), jnp.int32),
            jax.ShapeDtypeStruct((RING * PLANE, TILE), F32),
            jax.ShapeDtypeStruct((RING * PLANE, TILE), F32),
            jax.ShapeDtypeStruct((1,), jnp.int32),
        ],
        scratch_shapes=[
            pltpu.VMEM((RING, PLANE, CLASSES), jnp.int32),
            pltpu.VMEM((RING, PLANE, TILE), jnp.int32),
        ],
        name="places",
    )(segments, all_wide)


def body(coupling, modes, flexibility, widths, segments):
    device = lax.axis_index("row") * 16 + lax.axis_index("col")
    own_segments = lax.dynamic_slice_in_dim(segments, device, 1, 0)
    tiles, diag, all_wide = make_block(coupling, modes, flexibility, widths, own_segments)
    table, row_hot, col_hot, choice = places(segments, all_wide)
    ring, own, diags = lax.switch(
        choice[0], [functools.partial(exchange, cap) for cap in CAPS], table, tiles, diag
    )
    out = assemble(table, ring, own, diags, row_hot, col_hot)
    return out.reshape(ROW_TILES * TILE, COL_TILES * TILE)


def solution(mesh):
    both = ("row", "col")
    return jax.shard_map(
        body,
        mesh=mesh,
        in_specs=(P(both, None, None), P(both, None, None), P(both, None), P(both), P()),
        out_specs=P("row", "col"),
        check_vma=False,
    )
```
